32 devices in a mesh: frame: 8 (over y, x, core), space: 4 (over z).
Axes of the slice: x: 2, y: 2, z: 4, core: 2. Of those that a mesh axis runs over, the one named last changes fastest.
Arguments:
- grad_out: bfloat16 [16, 880, 2240], P('frame', 'space'), may hold values from -6 to 6
- conv_taps: float32 [3, 2240], replicated, may hold values from -3 to 3
- saved_queries: bfloat16 [16, 880, 2240], P('frame', 'space'), may hold values from -6 to 6
- saved_keys: bfloat16 [16, 880, 2240], P('frame', 'space'), may hold values from -30 to 30
- saved_values: bfloat16 [16, 880, 2240], P('frame', 'space'), may hold values from -8 to 8
Outputs:
- grad_queries: bfloat16 [16, 880, 2240], P('frame', 'space')
- grad_keys: bfloat16 [16, 880, 2240], P('frame', 'space')
- grad_values: bfloat16 [16, 880, 2240], P('frame', 'space')
The draws below stay inside these ranges and needn't reach their ends.
All inputs are finite; a program needn't handle non-finite values.
Results may differ from the reference program's by a relative error of at most 0.015.
Values may be sent and summed in bfloat16 or wider, within the bound.
No kernel may reach another device: no remote copies, remote signals or barrier semaphores. Data moves between devices by JAX's collectives and lax.ppermute only.
A program may use at most 128 MiB of HBM per device.

```python
import math
import jax
import jax.numpy as jnp
from jax import lax

H = 20
E = 112
TOK = 880
C = 2240
FRAMES = 16


def draw_saved_keys(key, part):
    key_rows, key_cols, key_noise = jax.random.split(key, 3)
    shape_all = (FRAMES, TOK, H * E)
    row_scale = 10.0 ** jax.random.uniform(key_rows, (FRAMES, TOK, 1), minval=-0.5, maxval=0.5)
    col_scale = 10.0 ** jax.random.uniform(key_cols, (1, 1, H * E), minval=-0.5, maxval=0.5)
    ramp = jnp.arange(FRAMES, dtype=jnp.float32) / max(FRAMES - 1, 1)
    rising = (3.0 ** (ramp - 0.5))[:, None, None]
    base = jax.random.normal(key_noise, shape_all)
    values = jnp.clip(base * row_scale * col_scale * rising, -30.0, 30.0)
    return values.astype(jnp.bfloat16)


def draw_saved_values(key, part):
    own_key = jax.random.fold_in(key, 7193)
    key_noise = jax.random.fold_in(own_key, 0)
    shape_all = (FRAMES, TOK, H * E)
    noise = jax.random.normal(key_noise, shape_all)
    values = jnp.clip(noise, -8.0, 8.0)
    return values.astype(jnp.bfloat16)


def level_of(key, extent, shards, smallest, high):
    loudness, own = 1.0, jax.random.fold_in(key, 6)
    for position, blocks in shards:
        heights = jnp.exp(jax.random.uniform(jax.random.fold_in(own, position), (blocks,), jnp.float32, smallest / len(shards), high / len(shards)))
        loudness = loudness * jnp.repeat(heights, extent[position] // blocks).reshape([-1 if axis == position else 1 for axis in range(len(extent))])
    return loudness


def gaussian(key, extent, width, reach, pieces=(), kind=jnp.bfloat16):
    array = jax.random.normal(key, extent, jnp.float32) * width
    if len(pieces) > 0:
        array = level_of(key, extent, pieces, -0.22, 0.18) * array
    return jnp.clip(array, min=-reach, max=reach).astype(kind)


def setup_inputs(seed: int = 0) -> dict:
    keys = jax.random.split(jax.random.key(seed), 6)
    grad_out = gaussian(keys[0], (FRAMES, TOK, C), 1.0, 6.0, ((0, 8), (1, 4)))
    conv_taps = gaussian(keys[1], (3, C), 0.5, 3.0, (), jnp.float32)
    saved_queries = gaussian(keys[2], (FRAMES, TOK, C), 1.0, 6.0, ((0, 8), (1, 4)))
    saved_keys = draw_saved_keys(jax.random.fold_in(keys[5], 71), 0)
    saved_values = draw_saved_values(jax.random.fold_in(keys[5], 71), 0)
    return {"grad_out": grad_out, "conv_taps": conv_taps, "saved_queries": saved_queries, "saved_keys": saved_keys, "saved_values": saved_values}


EPSILON = 1e-06

def conv_transpose(grad_out, conv_taps):
    widened = grad_out.astype(jnp.float32)
    blanks = jnp.zeros_like(widened[:1])
    after_one = jnp.concatenate([widened[1:], blanks], 0)
    after_two = jnp.concatenate([widened[2:], blanks, blanks], 0)
    summed = widened * (1.0 + conv_taps[0]) + after_one * conv_taps[1] + after_two * conv_taps[2]
    return summed.astype(jnp.bfloat16)

def head_grads(bundle):
    queries, keys_in, values, upstream = bundle
    feat_query = jnp.maximum(queries, 0)
    feat_key = jnp.maximum(keys_in, 0)
    key_state = jnp.dot(feat_key.T, values, preferred_element_type=jnp.float32)
    key_total = lax.optimization_barrier(jnp.sum(feat_key.astype(jnp.float32), 0))
    state_half = key_state.astype(jnp.bfloat16)
    denominator = jnp.dot(feat_query.astype(jnp.float32), key_total, precision=lax.Precision.HIGHEST) + EPSILON
    numerator = jnp.dot(feat_query, state_half, preferred_element_type=jnp.float32)
    attended = numerator / denominator[:, None]
    grad_wide = upstream.astype(jnp.float32)
    grad_numer = (grad_wide / denominator[:, None]).astype(jnp.bfloat16)
    grad_denom = -lax.optimization_barrier(jnp.sum(grad_wide * attended, 1)) / denominator
    grad_state = jnp.dot(feat_query.T, grad_numer, preferred_element_type=jnp.float32)
    grad_total = jnp.dot(grad_denom, feat_query.astype(jnp.float32), precision=lax.Precision.HIGHEST)
    grad_half = grad_state.astype(jnp.bfloat16)
    query_part = jnp.dot(grad_numer, state_half.T, preferred_element_type=jnp.float32) + grad_denom[:, None] * key_total[None, :]
    key_part = jnp.dot(values, grad_half.T, preferred_element_type=jnp.float32) + grad_total[None, :]
    value_part = jnp.dot(feat_key, grad_half, preferred_element_type=jnp.float32)
    return (jnp.where(queries > 0, query_part, 0.0), jnp.where(keys_in > 0, key_part, 0.0), value_part)

def reference(grad_out, conv_taps, saved_queries, saved_keys, saved_values):
    upstream = conv_transpose(grad_out, conv_taps)
    token_count = FRAMES * TOK

    def to_heads(tensor):
        return jnp.transpose(tensor.reshape(token_count, H, E), (1, 0, 2))
    gradients = lax.map(head_grads, (to_heads(saved_queries), to_heads(saved_keys), to_heads(saved_values), to_heads(upstream)))
    loss_scale = 2.0 * math.sqrt(token_count)

    def from_heads(tensor):
        return (jnp.transpose(tensor, (1, 0, 2)).reshape(FRAMES, TOK, H * E) * loss_scale).astype(jnp.bfloat16)
    return (from_heads(gradients[0]), from_heads(gradients[1]), from_heads(gradients[2]))
```

```python
import functools
import math

import jax
import jax.numpy as jnp
from jax import lax
from jax.experimental import pallas as pl
from jax.experimental.pallas import tpu as pltpu
from jax.sharding import PartitionSpec as P

H = 20
E = 112
EPSILON = 1e-06
LANES = 128
SPAN = 256
ROWS = 14
PARTS = E // ROWS
COPY = 32
F32, BF16 = jnp.float32, jnp.bfloat16
PARAMS = pltpu.CompilerParams(vmem_limit_bytes=48 << 20)


def spans(width):
    blocks = []
    for start in range(0, width, SPAN):
        stop = min(start + SPAN, width)
        first, last = start // E, (stop - 1) // E
        low = first * E // LANES * LANES
        high = min(-(-(last + 1) * E // LANES) * LANES, width)
        blocks.append((start, stop, low, high, range(first, last + 1)))
    return blocks


def dot(a, b, contract):
    return lax.dot_general(a, b, ((contract[:1], contract[1:]), ((), ())), preferred_element_type=F32)


def head_of_lane(rows, start, stop):
    return (lax.broadcasted_iota(jnp.int32, (rows, stop - start), 1) + start) // E


def picks(start, stop):
    row = lax.broadcasted_iota(jnp.int32, (LANES, stop - start), 0)
    return (row % COPY == head_of_lane(LANES, start, stop)) & (row < 3 * COPY)


def split(x):
    high = x.astype(BF16)
    return high, (x - high.astype(F32)).astype(BF16)


def add_outer(state, left, right):
    for start, stop, low, high, heads in spans(left.shape[1]):
        product = dot(left[:, low:high], right[:, start:stop], (0, 0))
        owner = head_of_lane(E, start, stop)
        part = jnp.zeros((E, stop - start), F32)
        for h in heads:
            part = jnp.where(owner == h, product[h * E - low : (h + 1) * E - low], part)
        state[:, start:stop] += part


def write_messages(rank, state, total, sorted_ref, out_refs):
    high, low = split(total)
    for part in range(PARTS):
        rows = state[part * ROWS : (part + 1) * ROWS, :]
        sorted_ref[part] = jnp.concatenate([rows, high.astype(F32), low.astype(F32)], 0)
    for d, out in enumerate(out_refs):
        out[...] = sorted_ref[rank ^ d].astype(BF16)


def load_state(messages, state):
    for part in range(PARTS):
        state[part * ROWS : (part + 1) * ROWS, :] = messages[part].astype(F32)[:ROWS]


def read_totals(messages):
    rows = messages[0].astype(F32)
    return rows[ROWS : ROWS + 1], rows[ROWS + 1 : ROWS + 2]


def columns_of(state, block):
    start, stop, low, high, heads = block
    owner = head_of_lane(E, start, stop)
    rows = [jnp.where(owner == h, state[:, start:stop], 0.0) for h in heads]
    before, after = heads[0] * E - low, high - (heads[-1] + 1) * E
    if before > 0:
        rows = [jnp.zeros((before, stop - start), F32)] + rows
    if after > 0:
        rows = rows + [jnp.zeros((after, stop - start), F32)]
    return jnp.concatenate(rows, 0).astype(BF16)


def rows_of(state, block):
    start, stop, low, high, heads = block
    owner = head_of_lane(E, low, high)
    rows = []
    for h in heads:
        first, last = max(start - h * E, 0), min(stop - h * E, E)
        rows.append(jnp.where(owner[first:last] == h, state[first:last, low:high], 0.0))
    return jnp.concatenate(rows, 0).astype(BF16)


def key_kernel(rank_ref, keys_ref, values_ref, *refs):
    out_refs, (state, total, sorted_ref) = refs[:PARTS], refs[PARTS:]
    frame = pl.program_id(0)

    @pl.when(frame == 0)
    def _():
        state[...] = jnp.zeros_like(state)
        total[...] = jnp.zeros_like(total)

    feat = jnp.maximum(keys_ref[0], 0)
    add_outer(state, feat, values_ref[0])
    total[...] += dot(jnp.ones((8, feat.shape[0]), BF16), feat, (1, 0))

    @pl.when(frame == pl.num_programs(0) - 1)
    def _():
        write_messages(rank_ref[0], state[...], total[:1], sorted_ref, out_refs)


def sum_kernel(*refs):
    in_refs, out_ref = refs[:-1], refs[-1]
    added = in_refs[0][...].astype(F32)
    for ref in in_refs[1:]:
        added = added + ref[...].astype(F32)
    high, low = split(added[ROWS : ROWS + 1] + added[ROWS + 1 : ROWS + 2])
    row = lax.broadcasted_iota(jnp.int32, added.shape, 0)
    added = jnp.where(row == ROWS, high.astype(F32), added)
    added = jnp.where(row == ROWS + 1, low.astype(F32), added)
    out_ref[...] = added.astype(BF16)


def query_kernel(rank_ref, queries_ref, grad_ref, next_ref, taps_ref, messages_ref, *refs):
    numer_ref, denom_ref, *refs = refs
    out_refs, (state, total, sorted_ref, wide) = refs[:PARTS], refs[PARTS:]
    frames, tokens, width = queries_ref.shape
    load_state(messages_ref, state)
    tot_high, tot_low = read_totals(messages_ref)
    blocks = spans(width)
    taps = taps_ref[...]
    taps = [taps[0:1] + 1.0, taps[1:2], taps[2:3]]
    for i, block in enumerate(blocks):
        wide[i, : block[3] - block[2], : block[1] - block[0]] = columns_of(state, block)
    state[...] = jnp.zeros_like(state)
    total[...] = jnp.zeros_like(total)
    lane = lax.broadcasted_iota(jnp.int32, (tokens, LANES), 1)

    def frame_step(frame, following):
        feat = jnp.maximum(queries_ref[frame], 0)
        denominator = jnp.full((tokens, LANES), EPSILON, F32)
        for start, stop, *_ in blocks:
            pick = picks(start, stop)
            for tot in (tot_high, tot_low):
                weights = jnp.where(pick, tot[:, start:stop], 0.0).astype(BF16)
                denominator += dot(feat[:, start:stop], weights, (1, 1))
        inverse = jnp.where(lane % COPY < H, 1.0 / denominator, 0.0)
        high, rest = split(inverse)
        middle, low = split(inverse - high.astype(F32))
        spread = jnp.where(lane < COPY, high.astype(F32), jnp.where(lane < 2 * COPY, middle.astype(F32), low_part(inverse, high, middle)))
        spread = jnp.where(lane < 3 * COPY, spread, 0.0).astype(BF16)
        summed = jnp.zeros((tokens, LANES), F32)
        for i, (start, stop, low_lane, high_lane, _) in enumerate(blocks):
            pick = jnp.where(picks(start, stop), 1.0, 0.0).astype(BF16)
            upstream = grad_ref[frame, :, start:stop].astype(F32) * taps[0][:, start:stop]
            for tap, source in zip(taps[1:], following):
                upstream += source[:, start:stop].astype(F32) * tap[:, start:stop]
            upstream = upstream.astype(BF16).astype(F32)
            scaled = upstream * dot(spread, pick, (1, 0))
            numer_ref[frame, :, start:stop] = scaled.astype(BF16)
            attended = dot(feat[:, low_lane:high_lane], wide[i, : high_lane - low_lane, : stop - start], (1, 0))
            for part in split(scaled * attended):
                summed += dot(part, pick, (1, 1))
        grad_denom = -summed * inverse
        high, low = split(grad_denom)
        high, low = high.astype(F32), low.astype(F32)
        sides = jnp.where((lane >= COPY) & (lane < 2 * COPY), low, high)
        sides = jnp.where(lane < 3 * COPY, sides, 0.0)
        denom_ref[frame] = sides.astype(BF16)
        numer = numer_ref[frame]
        add_outer(state, feat, numer)
        pairs = jnp.where(lane < 2 * COPY, sides, 0.0).astype(BF16)
        for start, stop, *_ in blocks:
            terms = dot(pairs, feat[:, start:stop], (0, 0))
            total[:, start:stop] += jnp.sum(jnp.where(picks(start, stop), terms, 0.0), 0, keepdims=True)

    for frame in range(frames):
        following = [
            grad_ref.at[i] if i < frames else next_ref.at[i - frames] for i in (frame + 1, frame + 2)
        ]
        frame_step(frame, following)
    write_messages(rank_ref[0], state[...], total[...], sorted_ref, out_refs)


def low_part(whole, high, middle):
    return whole - high.astype(F32) - middle.astype(F32)


def query_grad_kernel(scale, queries_ref, numer_ref, denom_ref, messages_ref, out_ref, state, across):
    blocks = spans(queries_ref.shape[2])
    tot_high, tot_low = read_totals(messages_ref)

    @pl.when(pl.program_id(0) == 0)
    def _():
        load_state(messages_ref, state)
        for i, block in enumerate(blocks):
            across[i, : block[1] - block[0], : block[3] - block[2]] = rows_of(state, block)

    denom = denom_ref[0]
    for i, (start, stop, low, high, _) in enumerate(blocks):
        row = lax.broadcasted_iota(jnp.int32, (LANES, stop - start), 0)
        tot = jnp.where(row < 2 * COPY, tot_high[:, start:stop], tot_low[:, start:stop])
        tot = jnp.where(picks(start, stop), tot, 0.0).astype(BF16)
        grad = dot(numer_ref[0, :, low:high], across[i, : stop - start, : high - low], (1, 1)) + dot(denom, tot, (1, 0))
        alive = queries_ref[0, :, start:stop].astype(F32) > 0
        out_ref[0, :, start:stop] = jnp.where(alive, grad * scale, 0.0).astype(BF16)


def key_grad_kernel(scale, keys_ref, values_ref, messages_ref, key_out, value_out, state, across, wide):
    blocks = spans(keys_ref.shape[2])
    rows = messages_ref[0].astype(F32)
    row = lax.broadcasted_iota(jnp.int32, rows.shape, 0)
    total = jnp.sum(jnp.where(row >= ROWS, rows, 0.0), 0, keepdims=True)

    @pl.when(pl.program_id(0) == 0)
    def _():
        load_state(messages_ref, state)
        for i, block in enumerate(blocks):
            across[i, : block[1] - block[0], : block[3] - block[2]] = rows_of(state, block)
            wide[i, : block[3] - block[2], : block[1] - block[0]] = columns_of(state, block)

    feat = jnp.maximum(keys_ref[0], 0)
    for i, (start, stop, low, high, _) in enumerate(blocks):
        grad = dot(values_ref[0, :, low:high], across[i, : stop - start, : high - low], (1, 1)) + total[:, start:stop]
        alive = keys_ref[0, :, start:stop].astype(F32) > 0
        key_out[0, :, start:stop] = jnp.where(alive, grad * scale, 0.0).astype(BF16)
        grad = dot(feat[:, low:high], wide[i, : high - low, : stop - start], (1, 0))
        value_out[0, :, start:stop] = (grad * scale).astype(BF16)


def cost(flops, size):
    return pl.CostEstimate(flops=flops, bytes_accessed=size, transcendentals=0)


def exchange(block, axis, distance):
    devices = range(lax.axis_size(axis))
    return lax.ppermute(block, axis, [(i, i ^ distance) for i in devices])


def total_of(messages):
    width = messages[0].shape[1]

    def added(parts):
        return pl.pallas_call(
            sum_kernel,
            out_shape=jax.ShapeDtypeStruct(parts[0].shape, BF16),
            compiler_params=pltpu.CompilerParams(vmem_limit_bytes=8 << 20),
            cost_estimate=cost(0, 9 * 32 * width),
        )(*parts)

    frames = lax.axis_size("frame")
    with jax.named_scope("spread"):
        got = [exchange(messages[d], "frame", d) for d in range(1, PARTS)]
    part = added([messages[0], *got])
    steps = [("frame", PARTS * d) for d in range(1, frames // PARTS)]
    if steps:
        part = added([part] + [exchange(part, *step) for step in steps])
    steps = [("space", d) for d in range(1, lax.axis_size("space"))]
    if steps:
        part = added([part] + [exchange(part, *step) for step in steps])
    groups = [list(range(i, i + PARTS)) for i in range(0, frames, PARTS)]
    return lax.all_gather(part, "frame", axis_index_groups=groups if len(groups) > 1 else None)


def shards(grad_out, conv_taps, saved_queries, saved_keys, saved_values):
    frames, tokens, width = grad_out.shape
    devices = lax.axis_size("frame")
    rank = (lax.axis_index("frame") % PARTS).astype(jnp.int32).reshape(1)
    scale = 2.0 * math.sqrt(frames * devices * tokens * lax.axis_size("space"))
    array = jax.ShapeDtypeStruct(grad_out.shape, BF16)
    message = jax.ShapeDtypeStruct((ROWS + 2, width), BF16)
    smem = pl.BlockSpec(memory_space=pltpu.SMEM)
    per_frame = pl.BlockSpec((1, tokens, width), lambda i: (i, 0, 0))
    scratch = [
        pltpu.VMEM((E, width), F32),
        pltpu.VMEM((8, width), F32),
        pltpu.VMEM((PARTS, ROWS + 2, width), F32),
    ]

    window = max(block[3] - block[2] for block in spans(width))
    across = pltpu.VMEM((len(spans(width)), SPAN, window), BF16)
    wide = pltpu.VMEM((len(spans(width)), window, SPAN), BF16)

    def whole(shape):
        return pl.BlockSpec(shape, lambda i: (0,) * len(shape))

    size = 2 * frames * tokens * width
    state_messages = pl.pallas_call(
        key_kernel,
        grid=(frames,),
        in_specs=[smem, per_frame, per_frame],
        out_specs=[whole(message.shape)] * PARTS,
        out_shape=[message] * PARTS,
        scratch_shapes=scratch,
        compiler_params=PARAMS,
        cost_estimate=cost(size * 512, 2 * size),
    )(rank, saved_keys, saved_values)
    with jax.named_scope("halo"):
        source, state_messages = lax.optimization_barrier((grad_out, state_messages))
        following = lax.ppermute(source, "frame", [(i + 1, i) for i in range(devices - 1)])
    states = total_of(state_messages)
    numer, denom, *grad_messages = pl.pallas_call(
        query_kernel,
        in_specs=[smem] + [pl.BlockSpec(memory_space=pltpu.VMEM)] * 5,
        out_shape=[array, jax.ShapeDtypeStruct((frames, tokens, LANES), BF16)] + [message] * PARTS,
        scratch_shapes=[scratch[0], pltpu.VMEM((1, width), F32), scratch[2], wide],
        compiler_params=PARAMS,
        cost_estimate=cost(size * 2048, 4 * size),
    )(rank, saved_queries, grad_out, following, conv_taps, states)
    per_denom = pl.BlockSpec((1, tokens, LANES), lambda i: (i, 0, 0))
    grad_queries = pl.pallas_call(
        functools.partial(query_grad_kernel, scale),
        grid=(frames,),
        in_specs=[per_frame, per_frame, per_denom, whole(states.shape)],
        out_specs=per_frame,
        out_shape=array,
        scratch_shapes=[scratch[0], across],
        compiler_params=PARAMS,
        cost_estimate=cost(size * 512, 3 * size),
    )(saved_queries, numer, denom, states)
    grads = total_of(grad_messages)
    grad_keys, grad_values = pl.pallas_call(
        functools.partial(key_grad_kernel, scale),
        grid=(frames,),
        in_specs=[per_frame, per_frame, whole(grads.shape)],
        out_specs=[per_frame, per_frame],
        out_shape=[array, array],
        scratch_shapes=[scratch[0], across, wide],
        compiler_params=PARAMS,
        cost_estimate=cost(size * 1024, 4 * size),
    )(saved_keys, saved_values, grads)
    return grad_queries, grad_keys, grad_values


def solution(mesh):
    block = P("frame", "space", None)
    return jax.shard_map(
        shards,
        mesh=mesh,
        in_specs=(block, P(), block, block, block),
        out_specs=(block, block, block),
        check_vma=False,
    )
```

```python
import functools
import math

import jax
import jax.numpy as jnp
from jax import lax
from jax.experimental import pallas as pl
from jax.experimental.pallas import tpu as pltpu
from jax.sharding import PartitionSpec as P


H = 20
E = 112
EPSILON = 1e-06
LANES = 128
SPAN = 256
ROWS = 14
PARTS = E // ROWS
COPY = 32
F32, BF16 = jnp.float32, jnp.bfloat16
PARAMS = pltpu.CompilerParams(vmem_limit_bytes=48 << 20)


def spans(width):
    blocks = []
    for start in range(0, width, SPAN):
        stop = min(start + SPAN, width)
        first, last = start // E, (stop - 1) // E
        low = first * E // LANES * LANES
        high = min(-(-(last + 1) * E // LANES) * LANES, width)
        blocks.append((start, stop, low, high, range(first, last + 1)))
    return blocks


def dot(a, b, contract):
    return lax.dot_general(a, b, ((contract[:1], contract[1:]), ((), ())), preferred_element_type=F32)


def head_of_lane(rows, start, stop):
    return (lax.broadcasted_iota(jnp.int32, (rows, stop - start), 1) + start) // E


def picks(start, stop):
    row = lax.broadcasted_iota(jnp.int32, (LANES, stop - start), 0)
    return (row % COPY == head_of_lane(LANES, start, stop)) & (row < 3 * COPY)


def split(x):
    high = x.astype(BF16)
    return high, (x - high.astype(F32)).astype(BF16)


def add_outer(state, left, right):
    for start, stop, low, high, heads in spans(left.shape[1]):
        product = dot(left[:, low:high], right[:, start:stop], (0, 0))
        owner = head_of_lane(E, start, stop)
        part = jnp.zeros((E, stop - start), F32)
        for h in heads:
            part = jnp.where(owner == h, product[h * E - low : (h + 1) * E - low], part)
        state[:, start:stop] += part


def take(ref, start, stop):
    block = ref[:, :, start:stop]
    return block.reshape(block.shape[0] * block.shape[1], stop - start)


def put(ref, start, stop, rows):
    ref[:, :, start:stop] = rows.reshape(ref.shape[0], ref.shape[1], stop - start)


def write_messages(rank, state, total, sorted_ref, out_refs):
    high, low = split(total)
    for part in range(PARTS):
        rows = state[part * ROWS : (part + 1) * ROWS, :]
        sorted_ref[part] = jnp.concatenate([rows, high.astype(F32), low.astype(F32)], 0)
    for d, out in enumerate(out_refs):
        out[...] = sorted_ref[rank ^ d].astype(BF16)


def load_state(messages, state):
    for part in range(PARTS):
        state[part * ROWS : (part + 1) * ROWS, :] = messages[part].astype(F32)[:ROWS]


def read_totals(message):
    rows = message[...].astype(F32)
    return rows[ROWS : ROWS + 1], rows[ROWS + 1 : ROWS + 2]


def columns_of(state, block):
    start, stop, low, high, heads = block
    owner = head_of_lane(E, start, stop)
    rows = [jnp.where(owner == h, state[:, start:stop], 0.0) for h in heads]
    before, after = heads[0] * E - low, high - (heads[-1] + 1) * E
    if before > 0:
        rows = [jnp.zeros((before, stop - start), F32)] + rows
    if after > 0:
        rows = rows + [jnp.zeros((after, stop - start), F32)]
    return jnp.concatenate(rows, 0).astype(BF16)


def rows_of(state, block):
    start, stop, low, high, heads = block
    owner = head_of_lane(E, low, high)
    rows = []
    for h in heads:
        first, last = max(start - h * E, 0), min(stop - h * E, E)
        rows.append(jnp.where(owner[first:last] == h, state[first:last, low:high], 0.0))
    return jnp.concatenate(rows, 0).astype(BF16)


def key_kernel(rank_ref, keys_ref, values_ref, *refs):
    out_refs, (state, total, sorted_ref) = refs[:PARTS], refs[PARTS:]
    step = pl.program_id(0)

    @pl.when(step == 0)
    def _():
        state[...] = jnp.zeros_like(state)
        total[...] = jnp.zeros_like(total)

    width = keys_ref.shape[2]
    feat = jnp.maximum(take(keys_ref, 0, width), 0)
    add_outer(state, feat, take(values_ref, 0, width))
    total[...] += dot(jnp.ones((8, feat.shape[0]), BF16), feat, (1, 0))

    @pl.when(step == pl.num_programs(0) - 1)
    def _():
        write_messages(rank_ref[0], state[...], total[:1], sorted_ref, out_refs)


def sum_kernel(n_total, *refs):
    in_refs, out_ref = refs[:-1], refs[-1]
    in_refs, total_refs = in_refs[: len(in_refs) - n_total], in_refs[len(in_refs) - n_total :]
    added = in_refs[0][...].astype(F32)
    for ref in in_refs[1:]:
        added = added + ref[...].astype(F32)
    if total_refs:
        total = total_refs[0][:1]
    else:
        total = added[ROWS : ROWS + 1] + added[ROWS + 1 : ROWS + 2]
    high, low = split(total)
    row = lax.broadcasted_iota(jnp.int32, added.shape, 0)
    added = jnp.where(row == ROWS, high.astype(F32), added)
    added = jnp.where(row == ROWS + 1, low.astype(F32), added)
    out_ref[...] = added.astype(BF16)


def query_kernel(rank_ref, queries_ref, grad_ref, taps_ref, message_ref, *refs):
    n_next = len(refs) - PARTS - 4
    next_refs, (numer_ref, inverse_ref, *refs) = refs[:n_next], refs[n_next:]
    out_refs, (state, sorted_ref) = refs[:PARTS], refs[PARTS:]
    tokens, frames, width = queries_ref.shape
    rows = tokens * frames
    blocks = spans(width)
    tot_high, tot_low = read_totals(message_ref)
    taps = taps_ref[...]
    taps = [taps[0:1] + 1.0, taps[1:2], taps[2:3]]
    state[...] = jnp.zeros_like(state)
    feat = jnp.maximum(take(queries_ref, 0, width), 0)
    denominator = jnp.full((rows, LANES), EPSILON, F32)
    for start, stop, *_ in blocks:
        pick = picks(start, stop)
        for tot in (tot_high, tot_low):
            weights = jnp.where(pick, tot[:, start:stop], 0.0).astype(BF16)
            denominator += dot(feat[:, start:stop], weights, (1, 1))
    lane = lax.broadcasted_iota(jnp.int32, (rows, LANES), 1)
    inverse = jnp.where((lane % COPY < H) & (lane < 3 * COPY), 1.0 / denominator, 0.0)
    inverse_ref[...] = inverse
    high, _ = split(inverse)
    high = high.astype(F32)
    middle = (inverse - high).astype(BF16).astype(F32)
    spread = jnp.where(lane < COPY, high, jnp.where(lane < 2 * COPY, middle, inverse - high - middle)).astype(BF16)
    for start, stop, *_ in blocks:
        frame = lax.broadcasted_iota(jnp.int32, (rows, stop - start), 0) % frames
        now = take(grad_ref, start, stop).astype(F32)
        later = jnp.concatenate([take(ref, start, stop).astype(F32) for ref in next_refs], 0)
        upstream = now * taps[0][:, start:stop]
        for lag in (1, 2):
            shifted = pltpu.roll(later, frames - lag, 0) if lag < frames else later
            if lag < frames:
                shifted = jnp.where(frame + lag < frames, pltpu.roll(now, rows - lag, 0), shifted)
            upstream += shifted * taps[lag][:, start:stop]
        upstream = upstream.astype(BF16).astype(F32)
        pick = jnp.where(picks(start, stop), 1.0, 0.0).astype(BF16)
        numer_ref[:, start:stop] = (upstream * dot(spread, pick, (1, 0))).astype(BF16)
    add_outer(state, feat, numer_ref)
    write_messages(rank_ref[0], state[...], jnp.zeros((1, width), F32), sorted_ref, out_refs)


def query_grad_kernel(scale, rank_ref, queries_ref, numer_ref, inverse_ref, *refs):
    message_refs, (out_ref, total_ref, state, sorted_ref, wide, across) = refs[:PARTS], refs[PARTS:]
    tokens, frames, width = queries_ref.shape
    rows = tokens * frames
    blocks = spans(width)
    tot_high, tot_low = read_totals(message_refs[0])
    for d, ref in enumerate(message_refs):
        sorted_ref[rank_ref[0] ^ d] = ref[...].astype(F32)
    load_state(sorted_ref, state)
    for i, block in enumerate(blocks):
        wide[i, : block[3] - block[2], : block[1] - block[0]] = columns_of(state, block)
        across[i, : block[1] - block[0], : block[3] - block[2]] = rows_of(state, block)
    summed = jnp.zeros((rows, LANES), F32)
    for i, (start, stop, low, high, _) in enumerate(blocks):
        pick = jnp.where(picks(start, stop), 1.0, 0.0).astype(BF16)
        feat = jnp.maximum(take(queries_ref, low, high), 0)
        attended = dot(feat, wide[i, : high - low, : stop - start], (1, 0))
        for part in split(numer_ref[:, start:stop].astype(F32) * attended):
            summed += dot(part, pick, (1, 1))
    high, low = split(-summed * inverse_ref[...])
    high, low = high.astype(F32), low.astype(F32)
    lane = lax.broadcasted_iota(jnp.int32, (rows, LANES), 1)
    sides = jnp.where((lane >= COPY) & (lane < 2 * COPY), low, high)
    pairs = jnp.where(lane < 2 * COPY, sides, 0.0).astype(BF16)
    sides = sides.astype(BF16)
    for i, (start, stop, low, high, _) in enumerate(blocks):
        queries = take(queries_ref, start, stop)
        pick = picks(start, stop)
        terms = dot(pairs, jnp.maximum(queries, 0), (0, 0))
        terms = jnp.sum(jnp.where(pick, terms, 0.0), 0, keepdims=True)
        total_ref[:, start:stop] = jnp.broadcast_to(terms, (8, stop - start))
        row = lax.broadcasted_iota(jnp.int32, (LANES, stop - start), 0)
        tot = jnp.where(row < 2 * COPY, tot_high[:, start:stop], tot_low[:, start:stop])
        tot = jnp.where(pick, tot, 0.0).astype(BF16)
        grad = dot(numer_ref[:, low:high], across[i, : stop - start, : high - low], (1, 1)) + dot(sides, tot, (1, 0))
        put(out_ref, start, stop, jnp.where(queries.astype(F32) > 0, grad * scale, 0.0).astype(BF16))


def key_grad_kernel(scale, keys_ref, values_ref, messages_ref, key_out, value_out, state, wide, across):
    blocks = spans(keys_ref.shape[2])
    load_state(messages_ref, state)
    rows = messages_ref[0].astype(F32)
    for part in range(1, PARTS):
        rows = rows + messages_ref[part].astype(F32)
    row = lax.broadcasted_iota(jnp.int32, rows.shape, 0)
    total = jnp.sum(jnp.where(row >= ROWS, rows, 0.0), 0, keepdims=True)
    for i, block in enumerate(blocks):
        across[i, : block[1] - block[0], : block[3] - block[2]] = rows_of(state, block)
        wide[i, : block[3] - block[2], : block[1] - block[0]] = columns_of(state, block)
    for i, (start, stop, low, high, _) in enumerate(blocks):
        grad = dot(take(values_ref, low, high), across[i, : stop - start, : high - low], (1, 1)) + total[:, start:stop]
        alive = take(keys_ref, start, stop).astype(F32) > 0
        put(key_out, start, stop, jnp.where(alive, grad * scale, 0.0).astype(BF16))
        feat = jnp.maximum(take(keys_ref, low, high), 0)
        grad = dot(feat, wide[i, : high - low, : stop - start], (1, 0))
        put(value_out, start, stop, (grad * scale).astype(BF16))


def cost(flops, size):
    return pl.CostEstimate(flops=flops, bytes_accessed=size, transcendentals=0)


def exchange(block, axis, distance):
    devices = range(lax.axis_size(axis))
    return lax.ppermute(block, axis, [(i, i ^ distance) for i in devices])


def added(parts, total=None):
    totals = [] if total is None else [total]
    return pl.pallas_call(
        functools.partial(sum_kernel, len(totals)),
        out_shape=jax.ShapeDtypeStruct(parts[0].shape, BF16),
        compiler_params=pltpu.CompilerParams(vmem_limit_bytes=8 << 20),
        cost_estimate=cost(0, 9 * 32 * parts[0].shape[1]),
    )(*parts, *totals)


def spread_out(messages):
    got = []
    for d in range(1, PARTS):
        got.append(exchange(messages[d], "frame", d))
    return [messages[0], *got]


def over_groups(part):
    frames = lax.axis_size("frame")
    for axis, steps in (("frame", range(PARTS, frames, PARTS)), ("space", range(1, lax.axis_size("space")))):
        if steps:
            part = added([part] + [exchange(part, axis, d) for d in steps])
    return part


def shards(grad_out, conv_taps, saved_queries, saved_keys, saved_values):
    frames, tokens, width = grad_out.shape
    devices = lax.axis_size("frame")
    rank = (lax.axis_index("frame") % PARTS).astype(jnp.int32).reshape(1)
    scale = 2.0 * math.sqrt(frames * devices * tokens * lax.axis_size("space"))
    grad_out, saved_queries, saved_keys, saved_values = (
        x.transpose(1, 0, 2) for x in (grad_out, saved_queries, saved_keys, saved_values)
    )
    array = jax.ShapeDtypeStruct(grad_out.shape, BF16)
    message = jax.ShapeDtypeStruct((ROWS + 2, width), BF16)
    smem = pl.BlockSpec(memory_space=pltpu.SMEM)
    vmem = pl.BlockSpec(memory_space=pltpu.VMEM)
    window = max(block[3] - block[2] for block in spans(width))
    state = pltpu.VMEM((E, width), F32)
    ordered = pltpu.VMEM((PARTS, ROWS + 2, width), F32)
    across = pltpu.VMEM((len(spans(width)), SPAN, window), BF16)
    wide = pltpu.VMEM((len(spans(width)), window, SPAN), BF16)
    size = 2 * frames * tokens * width
    steps = 2 if tokens % 2 == 0 else 1
    per_step = pl.BlockSpec((tokens // steps, frames, width), lambda i: (i, 0, 0))

    def halo(source):
        return lax.ppermute(source, "frame", [(i + 1, i) for i in range(devices - 1)])

    early = tokens // 5
    following = [halo(grad_out[:early])]
    key = pl.pallas_call(
        key_kernel,
        grid=(steps,),
        in_specs=[smem, per_step, per_step],
        out_specs=[pl.BlockSpec(message.shape, lambda i: (0, 0))] * PARTS,
        out_shape=[message] * PARTS,
        scratch_shapes=[state, pltpu.VMEM((8, width), F32), ordered],
        compiler_params=PARAMS,
        cost_estimate=cost(size * 512, 2 * size),
    )
    state_messages = key(rank, saved_keys, saved_values)
    following.append(halo(grad_out[early:]))
    part = over_groups(added(spread_out(state_messages)))
    query = pl.pallas_call(
        query_kernel,
        in_specs=[smem] + [vmem] * (4 + len(following)),
        out_shape=[jax.ShapeDtypeStruct((frames * tokens, width), BF16), jax.ShapeDtypeStruct((frames * tokens, LANES), F32)] + [message] * PARTS,
        scratch_shapes=[state, ordered],
        compiler_params=PARAMS,
        cost_estimate=cost(size * 1024, 4 * size),
    )
    numer, inverse, *grad_messages = query(rank, saved_queries, grad_out, conv_taps, part, *following)
    states = spread_out([part] * PARTS)
    grad_parts = spread_out(grad_messages)
    query_grad = pl.pallas_call(
        functools.partial(query_grad_kernel, scale),
        in_specs=[smem] + [vmem] * (3 + PARTS),
        out_shape=[array, jax.ShapeDtypeStruct((8, width), F32)],
        scratch_shapes=[state, ordered, wide, across],
        compiler_params=PARAMS,
        cost_estimate=cost(size * 1024, 3 * size),
    )
    grad_queries, total = query_grad(rank, saved_queries, numer, inverse, *states)
    part = over_groups(added(grad_parts, total))
    groups = [list(range(i, i + PARTS)) for i in range(0, devices, PARTS)]
    grads = lax.all_gather(part, "frame", axis_index_groups=groups if len(groups) > 1 else None)
    grad_keys, grad_values = pl.pallas_call(
        functools.partial(key_grad_kernel, scale),
        out_shape=[array, array],
        scratch_shapes=[state, wide, across],
        compiler_params=PARAMS,
        cost_estimate=cost(size * 1024, 4 * size),
    )(saved_keys, saved_values, grads)
    return tuple(x.transpose(1, 0, 2) for x in (grad_queries, grad_keys, grad_values))


def solution(mesh):
    block = P("frame", "space", None)
    return jax.shard_map(
        shards,
        mesh=mesh,
        in_specs=(block, P(), block, block, block),
        out_specs=(block, block, block),
        check_vma=False,
    )
```

```python
import functools
import math

import jax
import jax.numpy as jnp
from jax import lax
from jax.experimental import pallas as pl
from jax.experimental.pallas import tpu as pltpu
from jax.sharding import PartitionSpec as P


H = 20
E = 112
EPSILON = 1e-06
LANES = 128
SPAN = 256
ROWS = 14
PARTS = E // ROWS
COPY = 32
F32, BF16 = jnp.float32, jnp.bfloat16
PARAMS = pltpu.CompilerParams(vmem_limit_bytes=24 << 20)


def spans(width):
    blocks = []
    for start in range(0, width, SPAN):
        stop = min(start + SPAN, width)
        first, last = start // E, (stop - 1) // E
        low = first * E // LANES * LANES
        high = min(-(-(last + 1) * E // LANES) * LANES, width)
        blocks.append((start, stop, low, high, range(first, last + 1)))
    return blocks


def dot(a, b, contract):
    return lax.dot_general(a, b, ((contract[:1], contract[1:]), ((), ())), preferred_element_type=F32)


def head_of_lane(rows, start, stop):
    lane = lax.broadcasted_iota(jnp.int32, (1, stop - start), 1) + start
    head = jnp.full((1, stop - start), start // E, jnp.int32)
    for h in range(start // E + 1, (stop - 1) // E + 1):
        head += (lane >= h * E).astype(jnp.int32)
    return jnp.broadcast_to(head, (rows, stop - start))


def picks(start, stop, rows=LANES):
    row = lax.broadcasted_iota(jnp.int32, (rows, 1), 0) & (LANES - 1)
    slot = jnp.where(row < 3 * COPY, row & (COPY - 1), -1)
    return jnp.broadcast_to(slot, (rows, stop - start)) == head_of_lane(rows, start, stop)


def split(x):
    high = x.astype(BF16)
    return high, (x - high.astype(F32)).astype(BF16)


def add_outer(state, left, right):
    for start, stop, low, high, heads in spans(left.shape[1]):
        product = dot(left[:, low:high], right[:, start:stop], (0, 0))
        owner = head_of_lane(E, start, stop)
        part = jnp.zeros((E, stop - start), F32)
        for h in heads:
            part = jnp.where(owner == h, product[h * E - low : (h + 1) * E - low], part)
        state[:, start:stop] += part


def take(ref, start, stop):
    block = ref[:, :, start:stop]
    return block.reshape(block.shape[0] * block.shape[1], stop - start)


def flat(ref):
    tokens, frames, width = ref.shape
    return ref.reshape(tokens * frames, width)


def relay_kernel(*refs):
    count = len(refs) // 2
    in_refs, out_refs, sems = refs[:count], refs[count : 2 * count], refs[2 * count]
    copies = [
        pltpu.make_async_copy(flat(source), target, sems.at[i])
        for i, (source, target) in enumerate(zip(in_refs, out_refs))
    ]
    for copy in copies:
        copy.start()
    for copy in copies:
        copy.wait()


class Leaving:
    def __init__(self, source, target, sems):
        self.source, self.target, self.sems, self.copies, self.held = source, flat(target), sems, [], None

    def put(self, start, stop, rows):
        self.source[:, start:stop] = rows
        held, self.held = self.held, (start, stop)
        if held:
            self.send(*held)

    def send(self, start, stop):
        copy = pltpu.make_async_copy(
            self.source.at[:, start:stop], self.target.at[:, start:stop], self.sems.at[len(self.copies)]
        )
        copy.start()
        self.copies.append(copy)

    def finish(self):
        self.send(*self.held)
        for copy in self.copies:
            copy.wait()


def write_messages(rank, state, total, sorted_ref, out_refs):
    high, low = split(total)
    for part in range(PARTS):
        rows = state[part * ROWS : (part + 1) * ROWS, :]
        sorted_ref[part] = jnp.concatenate([rows, high.astype(F32), low.astype(F32)], 0)
    for d, out in enumerate(out_refs):
        out[...] = sorted_ref[rank ^ d].astype(BF16)


def load_state(messages, state):
    for part in range(PARTS):
        state[part * ROWS : (part + 1) * ROWS, :] = messages[part].astype(F32)[:ROWS]


def read_totals(message):
    rows = message[...].astype(F32)
    return rows[ROWS : ROWS + 1], rows[ROWS + 1 : ROWS + 2]


def columns_of(state, block):
    start, stop, low, high, heads = block
    owner = head_of_lane(E, start, stop)
    rows = [jnp.where(owner == h, state[:, start:stop], 0.0) for h in heads]
    before, after = heads[0] * E - low, high - (heads[-1] + 1) * E
    if before > 0:
        rows = [jnp.zeros((before, stop - start), F32)] + rows
    if after > 0:
        rows = rows + [jnp.zeros((after, stop - start), F32)]
    return jnp.concatenate(rows, 0).astype(BF16)


def rows_of(state, block):
    start, stop, low, high, heads = block
    owner = head_of_lane(E, low, high)
    rows = []
    for h in heads:
        first, last = max(start - h * E, 0), min(stop - h * E, E)
        rows.append(jnp.where(owner[first:last] == h, state[first:last, low:high], 0.0))
    return jnp.concatenate(rows, 0).astype(BF16)


def key_kernel(rank_ref, keys_ref, values_ref, *refs):
    out_refs, (state, total, sorted_ref) = refs[:PARTS], refs[PARTS:]
    step = pl.program_id(0)

    @pl.when(step == 0)
    def _():
        state[...] = jnp.zeros_like(state)
        total[...] = jnp.zeros_like(total)

    width = keys_ref.shape[2]
    feat = jnp.maximum(take(keys_ref, 0, width), 0)
    add_outer(state, feat, take(values_ref, 0, width))
    total[...] += dot(jnp.ones((8, feat.shape[0]), BF16), feat, (1, 0))

    @pl.when(step == pl.num_programs(0) - 1)
    def _():
        write_messages(rank_ref[0], state[...], total[:1], sorted_ref, out_refs)


def sum_kernel(n_total, *refs):
    in_refs, out_ref = refs[:-1], refs[-1]
    in_refs, total_refs = in_refs[: len(in_refs) - n_total], in_refs[len(in_refs) - n_total :]
    added = in_refs[0][...].astype(F32)
    for ref in in_refs[1:]:
        added = added + ref[...].astype(F32)
    if total_refs:
        total = total_refs[0][:1]
    else:
        total = added[ROWS : ROWS + 1] + added[ROWS + 1 : ROWS + 2]
    high, low = split(total)
    row = lax.broadcasted_iota(jnp.int32, added.shape, 0)
    added = jnp.where(row == ROWS, high.astype(F32), added)
    added = jnp.where(row == ROWS + 1, low.astype(F32), added)
    out_ref[...] = added.astype(BF16)


def query_kernel(frames, rank_ref, queries_ref, grad_ref, taps_ref, message_ref, *refs):
    n_next = len(refs) - PARTS - 6
    next_refs, (numer_ref, inverse_ref, *refs) = refs[:n_next], refs[n_next:]
    out_refs, (state, sorted_ref, next_ref, sems) = refs[:PARTS], refs[PARTS:]
    rows, width = queries_ref.shape
    blocks = spans(width)
    arrivals = []
    for i, (start, stop, *_) in enumerate(blocks):
        first, copies = 0, []
        for j, source in enumerate(next_refs):
            source = flat(source)
            last = first + source.shape[0]
            target = next_ref.at[first:last, start:stop]
            copies.append(pltpu.make_async_copy(source.at[:, start:stop], target, sems.at[j, i]))
            copies[-1].start()
            first = last
        arrivals.append(copies)
    tot_high, tot_low = read_totals(message_ref)
    taps = taps_ref[...]
    taps = [taps[0:1] + 1.0, taps[1:2], taps[2:3]]
    state[...] = jnp.zeros_like(state)
    denominator = jnp.zeros((rows, 2 * LANES), F32)
    for start, stop, *_ in blocks:
        row = lax.broadcasted_iota(jnp.int32, (2 * LANES, stop - start), 0)
        tot = jnp.where(row < LANES, tot_high[:, start:stop], tot_low[:, start:stop])
        weights = jnp.where(picks(start, stop, 2 * LANES), tot, 0.0).astype(BF16)
        denominator += dot(jnp.maximum(queries_ref[:, start:stop], 0), weights, (1, 1))
    denominator = denominator[:, :LANES] + denominator[:, LANES:] + EPSILON
    lane = lax.broadcasted_iota(jnp.int32, (rows, LANES), 1)
    inverse = jnp.where(((lane & (COPY - 1)) < H) & (lane < 3 * COPY), 1.0 / denominator, 0.0)
    inverse_ref[...] = inverse
    high = inverse.astype(BF16).astype(F32)
    middle = (inverse - high).astype(BF16).astype(F32)
    spread = jnp.where(lane < COPY, high, jnp.where(lane < 2 * COPY, middle, inverse - high - middle)).astype(BF16)
    frame_of_row = lax.broadcasted_iota(jnp.int32, (rows, 1), 0) % frames
    for i, (start, stop, *_) in enumerate(blocks):
        for copy in arrivals[i]:
            copy.wait()
        frame = jnp.broadcast_to(frame_of_row, (rows, stop - start))
        now = grad_ref[:, start:stop].astype(F32)
        later = next_ref[:, start:stop].astype(F32)
        upstream = now * taps[0][:, start:stop]
        for lag in (1, 2):
            shifted = pltpu.roll(later, frames - lag, 0) if lag < frames else later
            if lag < frames:
                shifted = jnp.where(frame + lag < frames, pltpu.roll(now, rows - lag, 0), shifted)
            upstream += shifted * taps[lag][:, start:stop]
        upstream = upstream.astype(BF16).astype(F32)
        pick = jnp.where(picks(start, stop), 1.0, 0.0).astype(BF16)
        numer_ref[:, start:stop] = (upstream * dot(spread, pick, (1, 0))).astype(BF16)
    add_outer(state, jnp.maximum(queries_ref[...], 0), numer_ref)
    write_messages(rank_ref[0], state[...], jnp.zeros((1, width), F32), sorted_ref, out_refs)


def query_grad_kernel(scale, rank_ref, queries_ref, numer_ref, inverse_ref, *refs):
    message_refs, refs = refs[:PARTS], refs[PARTS:]
    out_ref, total_ref, state, sorted_ref, wide, across, held, sems = refs
    rows, width = queries_ref.shape
    blocks = spans(width)
    tot_high, tot_low = read_totals(message_refs[0])
    for d, ref in enumerate(message_refs):
        sorted_ref[rank_ref[0] ^ d] = ref[...].astype(F32)
    load_state(sorted_ref, state)
    for i, block in enumerate(blocks):
        wide[i, : block[3] - block[2], : block[1] - block[0]] = columns_of(state, block)
        across[i, : block[1] - block[0], : block[3] - block[2]] = rows_of(state, block)
    summed = jnp.zeros((rows, LANES), F32)
    for i, (start, stop, low, high, _) in enumerate(blocks):
        pick = jnp.where(picks(start, stop), 1.0, 0.0).astype(BF16)
        feat = jnp.maximum(queries_ref[:, low:high], 0)
        attended = dot(feat, wide[i, : high - low, : stop - start], (1, 0))
        summed += dot((numer_ref[:, start:stop].astype(F32) * attended).astype(BF16), pick, (1, 1))
    high, low = split(-summed * inverse_ref[...])
    high, low = high.astype(F32), low.astype(F32)
    lane = lax.broadcasted_iota(jnp.int32, (rows, LANES), 1)
    sides = jnp.where((lane >= COPY) & (lane < 2 * COPY), low, high)
    pairs = jnp.where(lane < 2 * COPY, sides, 0.0).astype(BF16)
    sides = sides.astype(BF16)
    leaving = Leaving(held, out_ref, sems)
    for i, (start, stop, low, high, _) in enumerate(blocks):
        queries = queries_ref[:, start:stop]
        pick = picks(start, stop)
        terms = dot(pairs, jnp.maximum(queries, 0), (0, 0))
        terms = jnp.sum(jnp.where(pick, terms, 0.0), 0, keepdims=True)
        total_ref[:, start:stop] = jnp.broadcast_to(terms, (8, stop - start))
        row = lax.broadcasted_iota(jnp.int32, (LANES, stop - start), 0)
        tot = jnp.where(row < 2 * COPY, tot_high[:, start:stop], tot_low[:, start:stop])
        tot = jnp.where(pick, tot, 0.0).astype(BF16)
        grad = dot(numer_ref[:, low:high], across[i, : stop - start, : high - low], (1, 1)) + dot(sides, tot, (1, 0))
        leaving.put(start, stop, jnp.where(queries.astype(F32) > 0, grad * scale, 0.0).astype(BF16))
    leaving.finish()


def key_grad_kernel(scale, keys_ref, values_ref, messages_ref, key_out, value_out, *refs):
    state, wide, across, key_held, value_held, key_sems, value_sems = refs
    blocks = spans(keys_ref.shape[1])
    load_state(messages_ref, state)
    rows = messages_ref[0].astype(F32)
    for part in range(1, PARTS):
        rows = rows + messages_ref[part].astype(F32)
    row = lax.broadcasted_iota(jnp.int32, rows.shape, 0)
    total = jnp.sum(jnp.where(row >= ROWS, rows, 0.0), 0, keepdims=True)
    key_leaving = Leaving(key_held, key_out, key_sems)
    value_leaving = Leaving(value_held, value_out, value_sems)
    for i, block in enumerate(blocks):
        start, stop, low, high, _ = block
        across[i, : stop - start, : high - low] = rows_of(state, block)
        wide[i, : high - low, : stop - start] = columns_of(state, block)
        grad = dot(values_ref[:, low:high], across[i, : stop - start, : high - low], (1, 1)) + total[:, start:stop]
        alive = keys_ref[:, start:stop].astype(F32) > 0
        key_leaving.put(start, stop, jnp.where(alive, grad * scale, 0.0).astype(BF16))
        feat = jnp.maximum(keys_ref[:, low:high], 0)
        grad = dot(feat, wide[i, : high - low, : stop - start], (1, 0))
        value_leaving.put(start, stop, (grad * scale).astype(BF16))
    key_leaving.finish()
    value_leaving.finish()


def cost(flops, size):
    return pl.CostEstimate(flops=flops, bytes_accessed=size, transcendentals=0)


def exchange(block, axis, distance):
    devices = range(lax.axis_size(axis))
    return lax.ppermute(block, axis, [(i, i ^ distance) for i in devices])


def added(parts, total=None):
    totals = [] if total is None else [total]
    return pl.pallas_call(
        functools.partial(sum_kernel, len(totals)),
        out_shape=jax.ShapeDtypeStruct(parts[0].shape, BF16),
        compiler_params=pltpu.CompilerParams(vmem_limit_bytes=8 << 20),
        cost_estimate=cost(0, 9 * 32 * parts[0].shape[1]),
    )(*parts, *totals)


def spread_out(messages):
    got = []
    for d in range(1, PARTS):
        got.append(exchange(messages[d], "frame", d))
    return [messages[0], *got]


def over_groups(part):
    frames = lax.axis_size("frame")
    for axis, steps in (("frame", range(PARTS, frames, PARTS)), ("space", range(1, lax.axis_size("space")))):
        got = []
        for d in steps:
            got.append(exchange(part, axis, d))
        if got:
            part = added([part, *got])
    return part


def shards(grad_out, conv_taps, saved_queries, saved_keys, saved_values):
    frames, tokens, width = grad_out.shape
    devices = lax.axis_size("frame")
    rank = (lax.axis_index("frame") % PARTS).astype(jnp.int32).reshape(1)
    scale = 2.0 * math.sqrt(frames * devices * tokens * lax.axis_size("space"))
    grad_out, saved_queries, saved_keys, saved_values = (
        x.transpose(1, 0, 2) for x in (grad_out, saved_queries, saved_keys, saved_values)
    )
    array = jax.ShapeDtypeStruct(grad_out.shape, BF16)
    message = jax.ShapeDtypeStruct((ROWS + 2, width), BF16)
    smem = pl.BlockSpec(memory_space=pltpu.SMEM)
    vmem = pl.BlockSpec(memory_space=pltpu.VMEM)
    window = max(block[3] - block[2] for block in spans(width))
    state = pltpu.VMEM((E, width), F32)
    ordered = pltpu.VMEM((PARTS, ROWS + 2, width), F32)
    across = pltpu.VMEM((len(spans(width)), SPAN, window), BF16)
    wide = pltpu.VMEM((len(spans(width)), window, SPAN), BF16)
    size = 2 * frames * tokens * width
    steps = 2 if tokens % 2 == 0 else 1
    per_step = pl.BlockSpec((tokens // steps, frames, width), lambda i: (i, 0, 0))

    anywhere = pl.BlockSpec(memory_space=pl.ANY)
    merged = jax.ShapeDtypeStruct((frames * tokens, width), BF16)
    held = pltpu.VMEM(merged.shape, BF16)
    sems = pltpu.SemaphoreType.DMA((len(spans(width)),))

    def relay(*sources):
        return pl.pallas_call(
            relay_kernel,
            in_specs=[anywhere] * len(sources),
            out_specs=[vmem] * len(sources),
            out_shape=[merged] * len(sources),
            scratch_shapes=[pltpu.SemaphoreType.DMA((len(sources),))],
            compiler_params=PARAMS,
            cost_estimate=cost(0, 2 * size * len(sources)),
        )(*sources)

    def halo(source):
        return lax.ppermute(source, "frame", [(i + 1, i) for i in range(devices - 1)])

    early = tokens * 2 // 5 // 8 * 8
    following = [halo(grad_out[:early])]
    key = pl.pallas_call(
        key_kernel,
        grid=(steps,),
        in_specs=[smem, per_step, per_step],
        out_specs=[pl.BlockSpec(message.shape, lambda i: (0, 0))] * PARTS,
        out_shape=[message] * PARTS,
        scratch_shapes=[state, pltpu.VMEM((8, width), F32), ordered],
        compiler_params=PARAMS,
        cost_estimate=cost(size * 512, 2 * size),
    )
    state_messages = key(rank, saved_keys, saved_values)
    following.append(halo(grad_out[early:]))
    query_rows, grad_rows = relay(saved_queries, grad_out)
    part = over_groups(added(spread_out(state_messages)))
    query = pl.pallas_call(
        functools.partial(query_kernel, frames),
        in_specs=[smem] + [vmem] * 4 + [anywhere] * len(following),
        out_shape=[merged, jax.ShapeDtypeStruct((frames * tokens, LANES), F32)] + [message] * PARTS,
        scratch_shapes=[state, ordered, held, pltpu.SemaphoreType.DMA((len(following), len(spans(width))))],
        compiler_params=PARAMS,
        cost_estimate=cost(size * 1024, 4 * size),
    )
    numer, inverse, *grad_messages = query(rank, query_rows, grad_rows, conv_taps, part, *following)
    states = spread_out([part] * PARTS)
    grad_parts = spread_out(grad_messages)
    query_grad = pl.pallas_call(
        functools.partial(query_grad_kernel, scale),
        in_specs=[smem] + [vmem] * (3 + PARTS),
        out_specs=[anywhere, vmem],
        out_shape=[array, jax.ShapeDtypeStruct((8, width), F32)],
        scratch_shapes=[state, ordered, wide, across, held, sems],
        compiler_params=PARAMS,
        cost_estimate=cost(size * 1024, 3 * size),
    )
    grad_queries, total = query_grad(rank, query_rows, numer, inverse, *states)
    key_rows, value_rows = relay(saved_keys, saved_values)
    part = over_groups(added(grad_parts, total))
    groups = [list(range(i, i + PARTS)) for i in range(0, devices, PARTS)]
    grads = lax.all_gather(part, "frame", axis_index_groups=groups if len(groups) > 1 else None)
    grad_keys, grad_values = pl.pallas_call(
        functools.partial(key_grad_kernel, scale),
        in_specs=[vmem] * 3,
        out_specs=[anywhere] * 2,
        out_shape=[array, array],
        scratch_shapes=[state, wide, across, held, held, sems, sems],
        compiler_params=PARAMS,
        cost_estimate=cost(size * 1024, 4 * size),
    )(key_rows, value_rows, grads)
    return tuple(x.transpose(1, 0, 2) for x in (grad_queries, grad_keys, grad_values))


def solution(mesh):
    block = P("frame", "space", None)
    return jax.shard_map(
        shards,
        mesh=mesh,
        in_specs=(block, P(), block, block, block),
        out_specs=(block, block, block),
        check_vma=False,
    )
```

```python
import functools
import math

import jax
import jax.numpy as jnp
from jax import lax
from jax.experimental import pallas as pl
from jax.experimental.pallas import tpu as pltpu
from jax.sharding import PartitionSpec as P


H = 20
E = 112
EPSILON = 1e-06
LANES = 128
SPAN = 256
ROWS = 14
PARTS = E // ROWS
COPY = 32
F32, BF16 = jnp.float32, jnp.bfloat16
LARGE = pltpu.CompilerParams(vmem_limit_bytes=60 << 20)
PARAMS = pltpu.CompilerParams(vmem_limit_bytes=24 << 20)


def spans(width):
    blocks = []
    for start in range(0, width, SPAN):
        stop = min(start + SPAN, width)
        first, last = start // E, (stop - 1) // E
        low = first * E // LANES * LANES
        high = min(-(-(last + 1) * E // LANES) * LANES, width)
        blocks.append((start, stop, low, high, range(first, last + 1)))
    return blocks


def dot(a, b, contract):
    return lax.dot_general(a, b, ((contract[:1], contract[1:]), ((), ())), preferred_element_type=F32)


def head_of_lane(rows, start, stop):
    lane = lax.broadcasted_iota(jnp.int32, (1, stop - start), 1) + start
    head = jnp.full((1, stop - start), start // E, jnp.int32)
    for h in range(start // E + 1, (stop - 1) // E + 1):
        head += (lane >= h * E).astype(jnp.int32)
    return jnp.broadcast_to(head, (rows, stop - start))


def picks(start, stop, rows=LANES):
    row = lax.broadcasted_iota(jnp.int32, (rows, 1), 0) & (LANES - 1)
    slot = jnp.where(row < 3 * COPY, row & (COPY - 1), -1)
    return jnp.broadcast_to(slot, (rows, stop - start)) == head_of_lane(rows, start, stop)


def split(x):
    high = x.astype(BF16)
    return high, (x - high.astype(F32)).astype(BF16)


def add_outer(state, left, right):
    for start, stop, low, high, heads in spans(left.shape[1]):
        product = dot(left[:, low:high], right[:, start:stop], (0, 0))
        owner = head_of_lane(E, start, stop)
        part = jnp.zeros((E, stop - start), F32)
        for h in heads:
            part = jnp.where(owner == h, product[h * E - low : (h + 1) * E - low], part)
        state[:, start:stop] += part


def flat(ref):
    tokens, frames, width = ref.shape
    return ref.reshape(tokens * frames, width)


def relay_kernel(*refs):
    count = len(refs) // 2
    in_refs, out_refs, sems = refs[:count], refs[count : 2 * count], refs[2 * count]
    copies = [
        pltpu.make_async_copy(flat(source), target, sems.at[i])
        for i, (source, target) in enumerate(zip(in_refs, out_refs))
    ]
    for copy in copies:
        copy.start()
    for copy in copies:
        copy.wait()


class Leaving:
    def __init__(self, source, target, sems):
        self.source, self.target, self.sems, self.copies, self.sent = source, flat(target), sems, [], 0

    def put(self, start, stop, rows, send):
        self.source[:, start:stop] = rows
        if send:
            columns = slice(self.sent, stop)
            copy = pltpu.make_async_copy(
                self.source.at[:, columns], self.target.at[:, columns], self.sems.at[len(self.copies)]
            )
            copy.start()
            self.copies.append(copy)
            self.sent = stop

    def finish(self):
        for copy in self.copies:
            copy.wait()


def last_of(i, count, pieces):
    return (i + 1) * pieces // count > i * pieces // count


def write_messages(rank, state, total, sorted_ref, out_refs):
    high, low = split(total)
    for part in range(PARTS):
        rows = state[part * ROWS : (part + 1) * ROWS, :]
        sorted_ref[part] = jnp.concatenate([rows, high.astype(F32), low.astype(F32)], 0)
    for d, out in enumerate(out_refs):
        out[...] = sorted_ref[rank ^ d].astype(BF16)


def load_state(messages, state):
    for part in range(PARTS):
        state[part * ROWS : (part + 1) * ROWS, :] = messages[part].astype(F32)[:ROWS]


def read_totals(message):
    rows = message[...].astype(F32)
    return rows[ROWS : ROWS + 1], rows[ROWS + 1 : ROWS + 2]


def columns_of(state, block):
    start, stop, low, high, heads = block
    owner = head_of_lane(E, start, stop)
    rows = [jnp.where(owner == h, state[:, start:stop], 0.0) for h in heads]
    before, after = heads[0] * E - low, high - (heads[-1] + 1) * E
    if before > 0:
        rows = [jnp.zeros((before, stop - start), F32)] + rows
    if after > 0:
        rows = rows + [jnp.zeros((after, stop - start), F32)]
    return jnp.concatenate(rows, 0).astype(BF16)


def rows_of(state, block):
    start, stop, low, high, heads = block
    owner = head_of_lane(E, low, high)
    rows = []
    for h in heads:
        first, last = max(start - h * E, 0), min(stop - h * E, E)
        rows.append(jnp.where(owner[first:last] == h, state[first:last, low:high], 0.0))
    return jnp.concatenate(rows, 0).astype(BF16)


def key_kernel(rank_ref, keys_ref, values_ref, *refs):
    out_refs, (state, total, sorted_ref, key_rows, value_rows, sems) = refs[:PARTS], refs[PARTS:]
    tokens, frames, _ = keys_ref.shape
    cuts = [0, tokens // 16 * 8, tokens]
    arrivals = []
    for first, last in zip(cuts, cuts[1:]):
        rows = slice(first * frames, last * frames)
        for source, target in ((keys_ref, key_rows), (values_ref, value_rows)):
            arrivals.append(pltpu.make_async_copy(flat(source).at[rows], target.at[rows], sems.at[len(arrivals)]))
            arrivals[-1].start()
    state[...] = jnp.zeros_like(state)
    total[...] = jnp.zeros_like(total)
    for i, (first, last) in enumerate(zip(cuts, cuts[1:])):
        rows = slice(first * frames, last * frames)
        for copy in arrivals[2 * i : 2 * i + 2]:
            copy.wait()
        feat = jnp.maximum(key_rows[rows], 0)
        add_outer(state, feat, value_rows.at[rows])
        total[...] += dot(jnp.ones((8, feat.shape[0]), BF16), feat, (1, 0))
    write_messages(rank_ref[0], state[...], total[:1], sorted_ref, out_refs)


def sum_kernel(n_total, *refs):
    in_refs, out_ref = refs[:-1], refs[-1]
    in_refs, total_refs = in_refs[: len(in_refs) - n_total], in_refs[len(in_refs) - n_total :]
    added = in_refs[0][...].astype(F32)
    for ref in in_refs[1:]:
        added = added + ref[...].astype(F32)
    if total_refs:
        total = total_refs[0][:1]
    else:
        total = added[ROWS : ROWS + 1] + added[ROWS + 1 : ROWS + 2]
    high, low = split(total)
    row = lax.broadcasted_iota(jnp.int32, added.shape, 0)
    added = jnp.where(row == ROWS, high.astype(F32), added)
    added = jnp.where(row == ROWS + 1, low.astype(F32), added)
    out_ref[...] = added.astype(BF16)


def denominator_kernel(queries_ref, message_ref, inverse_ref, spread_ref):
    rows, width = queries_ref.shape
    tot_high, tot_low = read_totals(message_ref)
    denominator = jnp.zeros((rows, 2 * LANES), F32)
    for start, stop, *_ in spans(width):
        row = lax.broadcasted_iota(jnp.int32, (2 * LANES, stop - start), 0)
        tot = jnp.where(row < LANES, tot_high[:, start:stop], tot_low[:, start:stop])
        weights = jnp.where(picks(start, stop, 2 * LANES), tot, 0.0).astype(BF16)
        denominator += dot(jnp.maximum(queries_ref[:, start:stop], 0), weights, (1, 1))
    denominator = denominator[:, :LANES] + denominator[:, LANES:] + EPSILON
    lane = lax.broadcasted_iota(jnp.int32, (rows, LANES), 1)
    inverse = jnp.where(((lane & (COPY - 1)) < H) & (lane < 3 * COPY), 1.0 / denominator, 0.0)
    inverse_ref[...] = inverse
    high = inverse.astype(BF16).astype(F32)
    middle = (inverse - high).astype(BF16).astype(F32)
    low = inverse - high - middle
    spread_ref[...] = jnp.where(lane < COPY, high, jnp.where(lane < 2 * COPY, middle, low)).astype(BF16)


def query_kernel(frames, rank_ref, queries_ref, grad_ref, taps_ref, spread_ref, source_ref, *refs):
    numer_ref, *refs = refs
    out_refs, (state, sorted_ref, next_ref, sems) = refs[:PARTS], refs[PARTS:]
    rows, width = queries_ref.shape
    blocks = spans(width)
    taps = taps_ref[...]
    taps = [taps[0:1] + 1.0, taps[1:2], taps[2:3]]
    state[...] = jnp.zeros_like(state)
    group = 8 if 8 % frames == 0 and rows % 8 == 0 else rows
    for i, (start, stop, *_) in enumerate(blocks):
        arrival = pltpu.make_async_copy(flat(source_ref).at[:, start:stop], next_ref.at[:, start:stop], sems.at[i])
        arrival.start()
        arrival.wait()
        shape = (rows // group, group, stop - start)
        frame = lax.broadcasted_iota(jnp.int32, shape, 1) % frames
        now = grad_ref[:, start:stop].astype(F32).reshape(shape)
        later = next_ref[:, start:stop].astype(F32).reshape(shape)
        upstream = now * taps[0][:, start:stop]
        for lag in (1, 2):
            shifted = later
            if lag < frames:
                mixed = jnp.where(frame >= lag, now, later)
                ahead, behind = pltpu.roll(mixed, group - lag, 1), pltpu.roll(mixed, frames - lag, 1)
                shifted = jnp.where(frame + lag < frames, ahead, behind)
            upstream += shifted * taps[lag][:, start:stop]
        upstream = upstream.reshape(rows, stop - start)
        pick = jnp.where(picks(start, stop), 1.0, 0.0).astype(BF16)
        numer_ref[:, start:stop] = (upstream * dot(spread_ref[...], pick, (1, 0))).astype(BF16)
    add_outer(state, jnp.maximum(queries_ref[...], 0), numer_ref)
    write_messages(rank_ref[0], state[...], jnp.zeros((1, width), F32), sorted_ref, out_refs)


def sort_messages(rank, message_refs, sorted_ref, state):
    for d, ref in enumerate(message_refs):
        sorted_ref[rank ^ d] = ref[...].astype(F32)
    load_state(sorted_ref, state)


def side_kernel(rank_ref, queries_ref, numer_ref, inverse_ref, *refs):
    message_refs, (sides_ref, total_ref, state, sorted_ref, wide) = refs[:PARTS], refs[PARTS:]
    rows, width = queries_ref.shape
    blocks = spans(width)
    sort_messages(rank_ref[0], message_refs, sorted_ref, state)
    for i, block in enumerate(blocks):
        wide[i, : block[3] - block[2], : block[1] - block[0]] = columns_of(state, block)
    summed = jnp.zeros((rows, LANES), F32)
    for i, (start, stop, low, high, _) in enumerate(blocks):
        pick = jnp.where(picks(start, stop), 1.0, 0.0).astype(BF16)
        feat = jnp.maximum(queries_ref[:, low:high], 0)
        attended = dot(feat, wide[i, : high - low, : stop - start], (1, 0))
        summed += dot((numer_ref[:, start:stop].astype(F32) * attended).astype(BF16), pick, (1, 1))
    high, low = split(-summed * inverse_ref[...])
    high, low = high.astype(F32), low.astype(F32)
    lane = lax.broadcasted_iota(jnp.int32, (rows, LANES), 1)
    sides = jnp.where((lane >= COPY) & (lane < 2 * COPY), low, high)
    pairs = jnp.where(lane < 2 * COPY, sides, 0.0).astype(BF16)
    sides_ref[...] = sides.astype(BF16)
    for start, stop, *_ in blocks:
        terms = dot(pairs, jnp.maximum(queries_ref[:, start:stop], 0), (0, 0))
        terms = jnp.sum(jnp.where(picks(start, stop), terms, 0.0), 0, keepdims=True)
        total_ref[:, start:stop] = jnp.broadcast_to(terms, (8, stop - start))


def query_grad_kernel(scale, rank_ref, queries_ref, numer_ref, sides_ref, *refs):
    message_refs, (out_ref, state, sorted_ref, across, held, sems) = refs[:PARTS], refs[PARTS:]
    blocks = spans(queries_ref.shape[1])
    tot_high, tot_low = read_totals(message_refs[0])
    sort_messages(rank_ref[0], message_refs, sorted_ref, state)
    for i, block in enumerate(blocks):
        across[i, : block[1] - block[0], : block[3] - block[2]] = rows_of(state, block)
    leaving = Leaving(held, out_ref, sems)
    for i, (start, stop, low, high, _) in enumerate(blocks):
        row = lax.broadcasted_iota(jnp.int32, (LANES, stop - start), 0)
        tot = jnp.where(row < 2 * COPY, tot_high[:, start:stop], tot_low[:, start:stop])
        tot = jnp.where(picks(start, stop), tot, 0.0).astype(BF16)
        grad = dot(numer_ref[:, low:high], across[i, : stop - start, : high - low], (1, 1))
        grad += dot(sides_ref[...], tot, (1, 0))
        grad = jnp.where(queries_ref[:, start:stop].astype(F32) > 0, grad * scale, 0.0).astype(BF16)
        leaving.put(start, stop, grad, last_of(i, len(blocks), 3))
    leaving.finish()


def key_grad_kernel(scale, keys_ref, values_ref, messages_ref, key_out, value_out, *refs):
    state, wide, across, key_held, value_held, key_sems, value_sems = refs
    blocks = spans(keys_ref.shape[1])
    load_state(messages_ref, state)
    rows = messages_ref[0].astype(F32)
    for part in range(1, PARTS):
        rows = rows + messages_ref[part].astype(F32)
    row = lax.broadcasted_iota(jnp.int32, rows.shape, 0)
    total = jnp.sum(jnp.where(row >= ROWS, rows, 0.0), 0, keepdims=True)
    key_leaving = Leaving(key_held, key_out, key_sems)
    value_leaving = Leaving(value_held, value_out, value_sems)
    for i, block in enumerate(blocks):
        start, stop, low, high, _ = block
        across[i, : stop - start, : high - low] = rows_of(state, block)
        wide[i, : high - low, : stop - start] = columns_of(state, block)
    for i, (start, stop, low, high, _) in enumerate(blocks):
        grad = dot(values_ref[:, low:high], across[i, : stop - start, : high - low], (1, 1)) + total[:, start:stop]
        alive = keys_ref[:, start:stop].astype(F32) > 0
        grad = jnp.where(alive, grad * scale, 0.0).astype(BF16)
        key_leaving.put(start, stop, grad, last_of(i, len(blocks), 2))
    for i, (start, stop, low, high, _) in enumerate(blocks):
        feat = jnp.maximum(keys_ref[:, low:high], 0)
        grad = dot(feat, wide[i, : high - low, : stop - start], (1, 0))
        value_leaving.put(start, stop, (grad * scale).astype(BF16), last_of(i, len(blocks), 3))
    key_leaving.finish()
    value_leaving.finish()


def cost(flops, size):
    return pl.CostEstimate(flops=flops, bytes_accessed=size, transcendentals=0)


def exchange(block, axis, distance):
    devices = range(lax.axis_size(axis))
    return lax.ppermute(block, axis, [(i, i ^ distance) for i in devices])


def added(parts, total=None):
    totals = [] if total is None else [total]
    return pl.pallas_call(
        functools.partial(sum_kernel, len(totals)),
        out_shape=jax.ShapeDtypeStruct(parts[0].shape, BF16),
        compiler_params=pltpu.CompilerParams(vmem_limit_bytes=8 << 20),
        cost_estimate=cost(0, 9 * 32 * parts[0].shape[1]),
    )(*parts, *totals)


def spread_out(messages):
    got = []
    for d in range(1, PARTS):
        got.append(exchange(messages[d], "frame", d))
    return [messages[0], *got]


def over_groups(part):
    frames = lax.axis_size("frame")
    for axis, steps in (("frame", range(PARTS, frames, PARTS)), ("space", range(1, lax.axis_size("space")))):
        got = []
        for d in steps:
            got.append(exchange(part, axis, d))
        if got:
            part = added([part, *got])
    return part


def shards(grad_out, conv_taps, saved_queries, saved_keys, saved_values):
    frames, tokens, width = grad_out.shape
    devices = lax.axis_size("frame")
    rank = (lax.axis_index("frame") % PARTS).astype(jnp.int32).reshape(1)
    scale = 2.0 * math.sqrt(frames * devices * tokens * lax.axis_size("space"))
    grad_out, saved_queries, saved_keys, saved_values = (
        x.transpose(1, 0, 2) for x in (grad_out, saved_queries, saved_keys, saved_values)
    )
    array = jax.ShapeDtypeStruct(grad_out.shape, BF16)
    message = jax.ShapeDtypeStruct((ROWS + 2, width), BF16)
    smem = pl.BlockSpec(memory_space=pltpu.SMEM)
    vmem = pl.BlockSpec(memory_space=pltpu.VMEM)
    window = max(block[3] - block[2] for block in spans(width))
    state = pltpu.VMEM((E, width), F32)
    ordered = pltpu.VMEM((PARTS, ROWS + 2, width), F32)
    across = pltpu.VMEM((len(spans(width)), SPAN, window), BF16)
    wide = pltpu.VMEM((len(spans(width)), window, SPAN), BF16)
    size = 2 * frames * tokens * width

    anywhere = pl.BlockSpec(memory_space=pl.ANY)
    merged = jax.ShapeDtypeStruct((frames * tokens, width), BF16)
    held = pltpu.VMEM(merged.shape, BF16)
    sems = pltpu.SemaphoreType.DMA((len(spans(width)),))

    def relay(*sources):
        return pl.pallas_call(
            relay_kernel,
            in_specs=[anywhere] * len(sources),
            out_specs=[vmem] * len(sources),
            out_shape=[merged] * len(sources),
            scratch_shapes=[pltpu.SemaphoreType.DMA((len(sources),))],
            compiler_params=PARAMS,
            cost_estimate=cost(0, 2 * size * len(sources)),
        )(*sources)

    key = pl.pallas_call(
        key_kernel,
        in_specs=[smem, anywhere, anywhere],
        out_specs=[vmem] * PARTS,
        out_shape=[message] * PARTS,
        scratch_shapes=[state, pltpu.VMEM((8, width), F32), ordered, held, held, pltpu.SemaphoreType.DMA((4,))],
        compiler_params=LARGE,
        cost_estimate=cost(size * 512, 2 * size),
    )
    state_messages = key(rank, saved_keys, saved_values)
    following = lax.ppermute(grad_out, "frame", [(i + 1, i) for i in range(devices - 1)])
    query_rows, grad_rows = relay(saved_queries, grad_out)
    part = over_groups(added(spread_out(state_messages)))
    per_head = (frames * tokens, LANES)
    denominators = pl.pallas_call(
        denominator_kernel,
        out_shape=[jax.ShapeDtypeStruct(per_head, F32), jax.ShapeDtypeStruct(per_head, BF16)],
        compiler_params=PARAMS,
        cost_estimate=cost(size * 128, size),
    )
    inverse, spread = denominators(query_rows, part)
    query = pl.pallas_call(
        functools.partial(query_kernel, frames),
        in_specs=[smem] + [vmem] * 4 + [anywhere],
        out_shape=[merged] + [message] * PARTS,
        scratch_shapes=[state, ordered, held, sems],
        compiler_params=PARAMS,
        cost_estimate=cost(size * 1024, 4 * size),
    )
    numer, *grad_messages = query(rank, query_rows, grad_rows, conv_taps, spread, following)
    states = spread_out([part] * PARTS)
    grad_parts = spread_out(grad_messages)
    side = pl.pallas_call(
        side_kernel,
        in_specs=[smem] + [vmem] * (3 + PARTS),
        out_shape=[jax.ShapeDtypeStruct(per_head, BF16), jax.ShapeDtypeStruct((8, width), F32)],
        scratch_shapes=[state, ordered, wide],
        compiler_params=PARAMS,
        cost_estimate=cost(size * 512, 2 * size),
    )
    sides, total = side(rank, query_rows, numer, inverse, *states)
    query_grad = pl.pallas_call(
        functools.partial(query_grad_kernel, scale),
        in_specs=[smem] + [vmem] * (3 + PARTS),
        out_specs=anywhere,
        out_shape=array,
        scratch_shapes=[state, ordered, across, held, sems],
        compiler_params=PARAMS,
        cost_estimate=cost(size * 512, 3 * size),
    )
    grad_queries = query_grad(rank, query_rows, numer, sides, *states)
    key_rows, value_rows = relay(saved_keys, saved_values)
    part = over_groups(added(grad_parts, total))
    groups = [list(range(i, i + PARTS)) for i in range(0, devices, PARTS)]
    grads = lax.all_gather(part, "frame", axis_index_groups=groups if len(groups) > 1 else None)
    grad_keys, grad_values = pl.pallas_call(
        functools.partial(key_grad_kernel, scale),
        in_specs=[vmem] * 3,
        out_specs=[anywhere] * 2,
        out_shape=[array, array],
        scratch_shapes=[state, wide, across, held, held, sems, sems],
        compiler_params=PARAMS,
        cost_estimate=cost(size * 1024, 4 * size),
    )(key_rows, value_rows, grads)
    return tuple(x.transpose(1, 0, 2) for x in (grad_queries, grad_keys, grad_values))


def solution(mesh):
    block = P("frame", "space", None)
    return jax.shard_map(
        shards,
        mesh=mesh,
        in_specs=(block, P(), block, block, block),
        out_specs=(block, block, block),
        check_vma=False,
    )
```

```python
import functools
import math

import jax
import jax.numpy as jnp
from jax import lax
from jax.experimental import pallas as pl
from jax.experimental.pallas import tpu as pltpu
from jax.sharding import PartitionSpec as P


H = 20
E = 112
EPSILON = 1e-06
LANES = 128
SPAN = 256
ROWS = 14
PARTS = E // ROWS
COPY = 32
F32, BF16 = jnp.float32, jnp.bfloat16
LARGE = pltpu.CompilerParams(vmem_limit_bytes=60 << 20)
PARAMS = pltpu.CompilerParams(vmem_limit_bytes=24 << 20)


def spans(width):
    blocks = []
    for start in range(0, width, SPAN):
        stop = min(start + SPAN, width)
        first, last = start // E, (stop - 1) // E
        low = first * E // LANES * LANES
        high = min(-(-(last + 1) * E // LANES) * LANES, width)
        blocks.append((start, stop, low, high, range(first, last + 1)))
    return blocks


def dot(a, b, contract):
    return lax.dot_general(a, b, ((contract[:1], contract[1:]), ((), ())), preferred_element_type=F32)


def head_of_lane(rows, start, stop):
    lane = lax.broadcasted_iota(jnp.int32, (1, stop - start), 1) + start
    head = jnp.full((1, stop - start), start // E, jnp.int32)
    for h in range(start // E + 1, (stop - 1) // E + 1):
        head += (lane >= h * E).astype(jnp.int32)
    return jnp.broadcast_to(head, (rows, stop - start))


def picks(start, stop, rows=LANES):
    row = lax.broadcasted_iota(jnp.int32, (rows, 1), 0) & (LANES - 1)
    slot = jnp.where(row < 3 * COPY, row & (COPY - 1), -1)
    return jnp.broadcast_to(slot, (rows, stop - start)) == head_of_lane(rows, start, stop)


def split(x):
    high = x.astype(BF16)
    return high, (x - high.astype(F32)).astype(BF16)


def add_outer(state, left, right):
    for start, stop, low, high, heads in spans(left.shape[1]):
        product = dot(left[:, low:high], right[:, start:stop], (0, 0))
        owner = head_of_lane(E, start, stop)
        part = jnp.zeros((E, stop - start), F32)
        for h in heads:
            part = jnp.where(owner == h, product[h * E - low : (h + 1) * E - low], part)
        state[:, start:stop] += part


def flat(ref):
    tokens, frames, width = ref.shape
    return ref.reshape(tokens * frames, width)


def relay_kernel(*refs):
    count = len(refs) // 2
    in_refs, out_refs, sems = refs[:count], refs[count : 2 * count], refs[2 * count]
    copies = [
        pltpu.make_async_copy(flat(source), target, sems.at[i])
        for i, (source, target) in enumerate(zip(in_refs, out_refs))
    ]
    for copy in copies:
        copy.start()
    for copy in copies:
        copy.wait()


class Leaving:
    def __init__(self, source, target, sems):
        self.source, self.target, self.sems, self.copies, self.sent = source, flat(target), sems, [], 0

    def put(self, start, stop, rows, send):
        self.source[:, start:stop] = rows
        if send:
            columns = slice(self.sent, stop)
            copy = pltpu.make_async_copy(
                self.source.at[:, columns], self.target.at[:, columns], self.sems.at[len(self.copies)]
            )
            copy.start()
            self.copies.append(copy)
            self.sent = stop

    def finish(self):
        for copy in self.copies:
            copy.wait()


def last_of(i, count, pieces):
    return (i + 1) * pieces // count > i * pieces // count


def write_messages(rank, state, total, sorted_ref, out_refs):
    high, low = split(total)
    for part in range(PARTS):
        rows = state[part * ROWS : (part + 1) * ROWS, :]
        sorted_ref[part] = jnp.concatenate([rows, high.astype(F32), low.astype(F32)], 0)
    for k, out in enumerate(out_refs):
        for i in range(PARTS // 2):
            out[i] = sorted_ref[rank ^ (2 * i + k)].astype(BF16)


def load_state(messages, state):
    for part in range(PARTS):
        state[part * ROWS : (part + 1) * ROWS, :] = messages[part].astype(F32)[:ROWS]


def read_totals(message):
    rows = message[...].astype(F32)
    return rows[ROWS : ROWS + 1], rows[ROWS + 1 : ROWS + 2]


def columns_of(state, block):
    start, stop, low, high, heads = block
    owner = head_of_lane(E, start, stop)
    rows = [jnp.where(owner == h, state[:, start:stop], 0.0) for h in heads]
    before, after = heads[0] * E - low, high - (heads[-1] + 1) * E
    if before > 0:
        rows = [jnp.zeros((before, stop - start), F32)] + rows
    if after > 0:
        rows = rows + [jnp.zeros((after, stop - start), F32)]
    return jnp.concatenate(rows, 0).astype(BF16)


def rows_of(state, block):
    start, stop, low, high, heads = block
    owner = head_of_lane(E, low, high)
    rows = []
    for h in heads:
        first, last = max(start - h * E, 0), min(stop - h * E, E)
        rows.append(jnp.where(owner[first:last] == h, state[first:last, low:high], 0.0))
    return jnp.concatenate(rows, 0).astype(BF16)


def key_kernel(rank_ref, keys_ref, values_ref, *refs):
    out_refs, (state, total, sorted_ref, key_rows, value_rows, sems) = refs[:2], refs[2:]
    tokens, frames, _ = keys_ref.shape
    cuts = [0, tokens // 16 * 8, tokens]
    arrivals = []
    for first, last in zip(cuts, cuts[1:]):
        rows = slice(first * frames, last * frames)
        for source, target in ((keys_ref, key_rows), (values_ref, value_rows)):
            arrivals.append(pltpu.make_async_copy(flat(source).at[rows], target.at[rows], sems.at[len(arrivals)]))
            arrivals[-1].start()
    state[...] = jnp.zeros_like(state)
    total[...] = jnp.zeros_like(total)
    for i, (first, last) in enumerate(zip(cuts, cuts[1:])):
        rows = slice(first * frames, last * frames)
        for copy in arrivals[2 * i : 2 * i + 2]:
            copy.wait()
        feat = jnp.maximum(key_rows[rows], 0)
        add_outer(state, feat, value_rows.at[rows])
        total[...] += dot(jnp.ones((8, feat.shape[0]), BF16), feat, (1, 0))
    write_messages(rank_ref[0], state[...], total[:1], sorted_ref, out_refs)


def renewed(added, total):
    high, low = split(total)
    row = lax.broadcasted_iota(jnp.int32, added.shape, 0)
    added = jnp.where(row == ROWS, high.astype(F32), added)
    return jnp.where(row == ROWS + 1, low.astype(F32), added).astype(BF16)


def total_in(added):
    return added[ROWS : ROWS + 1] + added[ROWS + 1 : ROWS + 2]


def pair_kernel(own_ref, got_ref, *out_refs):
    for i, out in enumerate(out_refs):
        added = own_ref[i].astype(F32) + got_ref[i].astype(F32)
        out[...] = renewed(added, total_in(added))


def sum_kernel(n_total, *refs):
    in_refs, out_ref = refs[:-1], refs[-1]
    in_refs, total_refs = in_refs[: len(in_refs) - n_total], in_refs[len(in_refs) - n_total :]
    added = in_refs[0][...].astype(F32)
    for ref in in_refs[1:]:
        added = added + ref[...].astype(F32)
    out_ref[...] = renewed(added, total_refs[0][:1] if total_refs else total_in(added))


def stack_kernel(*refs):
    for i, ref in enumerate(refs[:-1]):
        refs[-1][i] = ref[...]


def denominator_kernel(queries_ref, message_ref, inverse_ref, spread_ref):
    rows, width = queries_ref.shape
    tot_high, tot_low = read_totals(message_ref)
    denominator = jnp.zeros((rows, 2 * LANES), F32)
    for start, stop, *_ in spans(width):
        row = lax.broadcasted_iota(jnp.int32, (2 * LANES, stop - start), 0)
        tot = jnp.where(row < LANES, tot_high[:, start:stop], tot_low[:, start:stop])
        weights = jnp.where(picks(start, stop, 2 * LANES), tot, 0.0).astype(BF16)
        denominator += dot(jnp.maximum(queries_ref[:, start:stop], 0), weights, (1, 1))
    denominator = denominator[:, :LANES] + denominator[:, LANES:] + EPSILON
    lane = lax.broadcasted_iota(jnp.int32, (rows, LANES), 1)
    inverse = jnp.where(((lane & (COPY - 1)) < H) & (lane < 3 * COPY), 1.0 / denominator, 0.0)
    inverse_ref[...] = inverse
    high = inverse.astype(BF16).astype(F32)
    middle = (inverse - high).astype(BF16).astype(F32)
    low = inverse - high - middle
    spread_ref[...] = jnp.where(lane < COPY, high, jnp.where(lane < 2 * COPY, middle, low)).astype(BF16)


def query_kernel(frames, rank_ref, queries_ref, grad_ref, taps_ref, spread_ref, *refs):
    source_refs, (numer_ref, *refs) = refs[:2], refs[2:]
    out_refs, (state, sorted_ref, next_ref, sems) = refs[:2], refs[2:]
    rows, width = queries_ref.shape
    blocks = spans(width)
    taps = taps_ref[...]
    taps = [taps[0:1] + 1.0, taps[1:2], taps[2:3]]
    state[...] = jnp.zeros_like(state)
    group = 8 if 8 % frames == 0 and rows % 8 == 0 else rows
    cuts, arrivals = sorted({0, 1, min(4, len(blocks)), len(blocks)}), {}
    for k, (begin, end) in enumerate(zip(cuts, cuts[1:])):
        columns, first = slice(blocks[begin][0], blocks[end - 1][1]), 0
        arrivals[begin] = []
        for j, source in enumerate(source_refs):
            last = first + source.shape[0] * frames
            target = next_ref.at[first:last, columns]
            copy = pltpu.make_async_copy(flat(source).at[:, columns], target, sems.at[j, k])
            copy.start()
            arrivals[begin].append(copy)
            first = last
    for i, (start, stop, *_) in enumerate(blocks):
        for copy in arrivals.get(i, ()):
            copy.wait()
        shape = (rows // group, group, stop - start)
        frame = lax.broadcasted_iota(jnp.int32, shape, 1) % frames
        now = grad_ref[:, start:stop].astype(F32).reshape(shape)
        later = next_ref[:, start:stop].astype(F32).reshape(shape)
        upstream = now * taps[0][:, start:stop]
        for lag in (1, 2):
            shifted = later
            if lag < frames:
                mixed = jnp.where(frame >= lag, now, later)
                ahead, behind = pltpu.roll(mixed, group - lag, 1), pltpu.roll(mixed, frames - lag, 1)
                shifted = jnp.where(frame + lag < frames, ahead, behind)
            upstream += shifted * taps[lag][:, start:stop]
        upstream = upstream.reshape(rows, stop - start)
        pick = jnp.where(picks(start, stop), 1.0, 0.0).astype(BF16)
        numer_ref[:, start:stop] = (upstream * dot(spread_ref[...], pick, (1, 0))).astype(BF16)
    add_outer(state, jnp.maximum(queries_ref[...], 0), numer_ref)
    write_messages(rank_ref[0], state[...], jnp.zeros((1, width), F32), sorted_ref, out_refs)


def sort_messages(rank, message_refs, sorted_ref, state):
    for k, stack in enumerate(message_refs):
        for i in range(PARTS // 2):
            sorted_ref[rank ^ (2 * i + k)] = stack[i].astype(F32)
    load_state(sorted_ref, state)


def side_kernel(rank_ref, queries_ref, numer_ref, inverse_ref, *refs):
    message_refs, (sides_ref, total_ref, state, sorted_ref, wide) = refs[:2], refs[2:]
    rows, width = queries_ref.shape
    blocks = spans(width)
    sort_messages(rank_ref[0], message_refs, sorted_ref, state)
    for i, block in enumerate(blocks):
        wide[i, : block[3] - block[2], : block[1] - block[0]] = columns_of(state, block)
    summed = jnp.zeros((rows, LANES), F32)
    for i, (start, stop, low, high, _) in enumerate(blocks):
        pick = jnp.where(picks(start, stop), 1.0, 0.0).astype(BF16)
        feat = jnp.maximum(queries_ref[:, low:high], 0)
        attended = dot(feat, wide[i, : high - low, : stop - start], (1, 0))
        summed += dot((numer_ref[:, start:stop].astype(F32) * attended).astype(BF16), pick, (1, 1))
    high, low = split(-summed * inverse_ref[...])
    high, low = high.astype(F32), low.astype(F32)
    lane = lax.broadcasted_iota(jnp.int32, (rows, LANES), 1)
    sides = jnp.where((lane >= COPY) & (lane < 2 * COPY), low, high)
    pairs = jnp.where(lane < 2 * COPY, sides, 0.0).astype(BF16)
    sides_ref[...] = sides.astype(BF16)
    for start, stop, *_ in blocks:
        terms = dot(pairs, jnp.maximum(queries_ref[:, start:stop], 0), (0, 0))
        terms = jnp.sum(jnp.where(picks(start, stop), terms, 0.0), 0, keepdims=True)
        total_ref[:, start:stop] = jnp.broadcast_to(terms, (8, stop - start))


def query_grad_kernel(scale, rank_ref, queries_ref, numer_ref, sides_ref, *refs):
    message_refs, (out_ref, state, sorted_ref, across, held, sems) = refs[:2], refs[2:]
    blocks = spans(queries_ref.shape[1])
    tot_high, tot_low = read_totals(message_refs[0].at[0])
    sort_messages(rank_ref[0], message_refs, sorted_ref, state)
    for i, block in enumerate(blocks):
        across[i, : block[1] - block[0], : block[3] - block[2]] = rows_of(state, block)
    leaving = Leaving(held, out_ref, sems)
    for i, (start, stop, low, high, _) in enumerate(blocks):
        row = lax.broadcasted_iota(jnp.int32, (LANES, stop - start), 0)
        tot = jnp.where(row < 2 * COPY, tot_high[:, start:stop], tot_low[:, start:stop])
        tot = jnp.where(picks(start, stop), tot, 0.0).astype(BF16)
        grad = dot(numer_ref[:, low:high], across[i, : stop - start, : high - low], (1, 1))
        grad += dot(sides_ref[...], tot, (1, 0))
        grad = jnp.where(queries_ref[:, start:stop].astype(F32) > 0, grad * scale, 0.0).astype(BF16)
        leaving.put(start, stop, grad, last_of(i, len(blocks), 3))
    leaving.finish()


def key_grad_kernel(scale, keys_ref, values_ref, messages_ref, key_out, value_out, *refs):
    state, wide, across, key_held, value_held, key_sems, value_sems = refs
    blocks = spans(keys_ref.shape[1])
    load_state(messages_ref, state)
    rows = messages_ref[0].astype(F32)
    for part in range(1, PARTS):
        rows = rows + messages_ref[part].astype(F32)
    row = lax.broadcasted_iota(jnp.int32, rows.shape, 0)
    total = jnp.sum(jnp.where(row >= ROWS, rows, 0.0), 0, keepdims=True)
    key_leaving = Leaving(key_held, key_out, key_sems)
    value_leaving = Leaving(value_held, value_out, value_sems)
    for i, block in enumerate(blocks):
        start, stop, low, high, _ = block
        across[i, : stop - start, : high - low] = rows_of(state, block)
        wide[i, : high - low, : stop - start] = columns_of(state, block)
    for i, (start, stop, low, high, _) in enumerate(blocks):
        grad = dot(values_ref[:, low:high], across[i, : stop - start, : high - low], (1, 1)) + total[:, start:stop]
        alive = keys_ref[:, start:stop].astype(F32) > 0
        grad = jnp.where(alive, grad * scale, 0.0).astype(BF16)
        key_leaving.put(start, stop, grad, last_of(i, len(blocks), 2))
    for i, (start, stop, low, high, _) in enumerate(blocks):
        feat = jnp.maximum(keys_ref[:, low:high], 0)
        grad = dot(feat, wide[i, : high - low, : stop - start], (1, 0))
        value_leaving.put(start, stop, (grad * scale).astype(BF16), last_of(i, len(blocks), 3))
    key_leaving.finish()
    value_leaving.finish()


def cost(flops, size):
    return pl.CostEstimate(flops=flops, bytes_accessed=size, transcendentals=0)


def exchange(block, axis, distance):
    devices = range(lax.axis_size(axis))
    return lax.ppermute(block, axis, [(i, i ^ distance) for i in devices])


def added(parts, total=None):
    totals = [] if total is None else [total]
    return pl.pallas_call(
        functools.partial(sum_kernel, len(totals)),
        out_shape=jax.ShapeDtypeStruct(parts[0].shape, BF16),
        compiler_params=pltpu.CompilerParams(vmem_limit_bytes=8 << 20),
        cost_estimate=cost(0, 9 * 32 * parts[0].shape[1]),
    )(*parts, *totals)


def small(kernel, out_shape, *arrays):
    return pl.pallas_call(
        kernel,
        out_shape=out_shape,
        compiler_params=pltpu.CompilerParams(vmem_limit_bytes=8 << 20),
        cost_estimate=cost(0, 4 * sum(x.size for x in arrays)),
    )(*arrays)


def fan(messages):
    got = [messages[0]]
    for i in range(1, PARTS // 2):
        got.append(exchange(messages[i], "frame", 2 * i))
    return got


def scattered(stacks):
    own, other = stacks
    got = exchange(other, "frame", 1)
    message = jax.ShapeDtypeStruct(own.shape[1:], BF16)
    return fan(small(pair_kernel, [message] * (PARTS // 2), own, got))


def gathered(part):
    parts = fan([part] * (PARTS // 2))
    own = small(stack_kernel, jax.ShapeDtypeStruct((len(parts), *part.shape), BF16), *parts)
    return own, exchange(own, "frame", 1)


def over_groups(part):
    frames = lax.axis_size("frame")
    for axis, steps in (("frame", range(PARTS, frames, PARTS)), ("space", range(1, lax.axis_size("space")))):
        got = []
        for d in steps:
            got.append(exchange(part, axis, d))
        if got:
            part = added([part, *got])
    return part


def shards(grad_out, conv_taps, saved_queries, saved_keys, saved_values):
    frames, tokens, width = grad_out.shape
    devices = lax.axis_size("frame")
    rank = (lax.axis_index("frame") % PARTS).astype(jnp.int32).reshape(1)
    scale = 2.0 * math.sqrt(frames * devices * tokens * lax.axis_size("space"))
    grad_out, saved_queries, saved_keys, saved_values = (
        x.transpose(1, 0, 2) for x in (grad_out, saved_queries, saved_keys, saved_values)
    )
    array = jax.ShapeDtypeStruct(grad_out.shape, BF16)
    stack = jax.ShapeDtypeStruct((PARTS // 2, ROWS + 2, width), BF16)
    smem = pl.BlockSpec(memory_space=pltpu.SMEM)
    vmem = pl.BlockSpec(memory_space=pltpu.VMEM)
    window = max(block[3] - block[2] for block in spans(width))
    state = pltpu.VMEM((E, width), F32)
    ordered = pltpu.VMEM((PARTS, ROWS + 2, width), F32)
    across = pltpu.VMEM((len(spans(width)), SPAN, window), BF16)
    wide = pltpu.VMEM((len(spans(width)), window, SPAN), BF16)
    size = 2 * frames * tokens * width

    anywhere = pl.BlockSpec(memory_space=pl.ANY)
    merged = jax.ShapeDtypeStruct((frames * tokens, width), BF16)
    held = pltpu.VMEM(merged.shape, BF16)
    sems = pltpu.SemaphoreType.DMA((len(spans(width)),))

    def relay(*sources):
        return pl.pallas_call(
            relay_kernel,
            in_specs=[anywhere] * len(sources),
            out_specs=[vmem] * len(sources),
            out_shape=[merged] * len(sources),
            scratch_shapes=[pltpu.SemaphoreType.DMA((len(sources),))],
            compiler_params=PARAMS,
            cost_estimate=cost(0, 2 * size * len(sources)),
        )(*sources)

    def halo(source):
        return lax.ppermute(source, "frame", [(i + 1, i) for i in range(devices - 1)])

    early = tokens * 1 // 2 // 8 * 8
    following = [halo(grad_out[:early])]
    key = pl.pallas_call(
        key_kernel,
        in_specs=[smem, anywhere, anywhere],
        out_specs=[vmem] * 2,
        out_shape=[stack] * 2,
        scratch_shapes=[state, pltpu.VMEM((8, width), F32), ordered, held, held, pltpu.SemaphoreType.DMA((4,))],
        compiler_params=LARGE,
        cost_estimate=cost(size * 512, 2 * size),
    )
    state_messages = key(rank, saved_keys, saved_values)
    following.append(halo(grad_out[early:]))
    query_rows, grad_rows = relay(saved_queries, grad_out)
    part = over_groups(added(scattered(state_messages)))
    per_head = (frames * tokens, LANES)
    denominators = pl.pallas_call(
        denominator_kernel,
        out_shape=[jax.ShapeDtypeStruct(per_head, F32), jax.ShapeDtypeStruct(per_head, BF16)],
        compiler_params=PARAMS,
        cost_estimate=cost(size * 128, size),
    )
    inverse, spread = denominators(query_rows, part)
    query = pl.pallas_call(
        functools.partial(query_kernel, frames),
        in_specs=[smem] + [vmem] * 4 + [anywhere] * 2,
        out_shape=[merged] + [stack] * 2,
        scratch_shapes=[state, ordered, held, pltpu.SemaphoreType.DMA((2, len(spans(width))))],
        compiler_params=PARAMS,
        cost_estimate=cost(size * 1024, 4 * size),
    )
    numer, *grad_messages = query(rank, query_rows, grad_rows, conv_taps, spread, *following)
    states = gathered(part)
    grad_parts = scattered(grad_messages)
    side = pl.pallas_call(
        side_kernel,
        in_specs=[smem] + [vmem] * 5,
        out_shape=[jax.ShapeDtypeStruct(per_head, BF16), jax.ShapeDtypeStruct((8, width), F32)],
        scratch_shapes=[state, ordered, wide],
        compiler_params=PARAMS,
        cost_estimate=cost(size * 512, 2 * size),
    )
    sides, total = side(rank, query_rows, numer, inverse, *states)
    query_grad = pl.pallas_call(
        functools.partial(query_grad_kernel, scale),
        in_specs=[smem] + [vmem] * 5,
        out_specs=anywhere,
        out_shape=array,
        scratch_shapes=[state, ordered, across, held, sems],
        compiler_params=PARAMS,
        cost_estimate=cost(size * 512, 3 * size),
    )
    grad_queries = query_grad(rank, query_rows, numer, sides, *states)
    key_rows, value_rows = relay(saved_keys, saved_values)
    part = over_groups(added(grad_parts, total))
    groups = [list(range(i, i + PARTS)) for i in range(0, devices, PARTS)]
    grads = lax.all_gather(part, "frame", axis_index_groups=groups if len(groups) > 1 else None)
    grad_keys, grad_values = pl.pallas_call(
        functools.partial(key_grad_kernel, scale),
        in_specs=[vmem] * 3,
        out_specs=[anywhere] * 2,
        out_shape=[array, array],
        scratch_shapes=[state, wide, across, held, held, sems, sems],
        compiler_params=PARAMS,
        cost_estimate=cost(size * 1024, 4 * size),
    )(key_rows, value_rows, grads)
    return tuple(x.transpose(1, 0, 2) for x in (grad_queries, grad_keys, grad_values))


def solution(mesh):
    block = P("frame", "space", None)
    return jax.shard_map(
        shards,
        mesh=mesh,
        in_specs=(block, P(), block, block, block),
        out_specs=(block, block, block),
        check_vma=False,
    )
```

```python
import functools
import math

import jax
import jax.numpy as jnp
from jax import lax
from jax.experimental import pallas as pl
from jax.experimental.pallas import tpu as pltpu
from jax.sharding import PartitionSpec as P


H = 20
E = 112
EPSILON = 1e-06
LANES = 128
SPAN = 256
ROWS = 14
PARTS = E // ROWS
COPY = 32
F32, BF16 = jnp.float32, jnp.bfloat16
LARGE = pltpu.CompilerParams(vmem_limit_bytes=57 << 20)
PARAMS = pltpu.CompilerParams(vmem_limit_bytes=24 << 20)


def spans(width):
    blocks = []
    for start in range(0, width, SPAN):
        stop = min(start + SPAN, width)
        first, last = start // E, (stop - 1) // E
        low = first * E // LANES * LANES
        high = min(-(-(last + 1) * E // LANES) * LANES, width)
        blocks.append((start, stop, low, high, range(first, last + 1)))
    return blocks


def dot(a, b, contract):
    return lax.dot_general(a, b, ((contract[:1], contract[1:]), ((), ())), preferred_element_type=F32)


def head_of_lane(rows, start, stop):
    lane = lax.broadcasted_iota(jnp.int32, (1, stop - start), 1) + start
    head = jnp.full((1, stop - start), start // E, jnp.int32)
    for h in range(start // E + 1, (stop - 1) // E + 1):
        head += (lane >= h * E).astype(jnp.int32)
    return jnp.broadcast_to(head, (rows, stop - start))


def picks(start, stop, rows=LANES):
    row = lax.broadcasted_iota(jnp.int32, (rows, 1), 0) & (LANES - 1)
    slot = jnp.where(row < 3 * COPY, row & (COPY - 1), -1)
    return jnp.broadcast_to(slot, (rows, stop - start)) == head_of_lane(rows, start, stop)


def split(x):
    high = x.astype(BF16)
    return high, (x - high.astype(F32)).astype(BF16)


def add_outer(state, left, right):
    for start, stop, low, high, heads in spans(left.shape[1]):
        product = dot(left[:, low:high], right[:, start:stop], (0, 0))
        owner = head_of_lane(E, start, stop)
        part = jnp.zeros((E, stop - start), F32)
        for h in heads:
            part = jnp.where(owner == h, product[h * E - low : (h + 1) * E - low], part)
        state[:, start:stop] += part


def flat(ref):
    tokens, frames, width = ref.shape
    return ref.reshape(tokens * frames, width)


def relay_kernel(*refs):
    count = len(refs) // 2
    in_refs, out_refs, sems = refs[:count], refs[count : 2 * count], refs[2 * count]
    copies = [
        pltpu.make_async_copy(flat(source), target, sems.at[i])
        for i, (source, target) in enumerate(zip(in_refs, out_refs))
    ]
    for copy in copies:
        copy.start()
    for copy in copies:
        copy.wait()


class Leaving:
    def __init__(self, source, target, sems):
        self.source, self.target, self.sems, self.copies, self.sent = source, flat(target), sems, [], 0

    def put(self, start, stop, rows, send):
        self.source[:, start:stop] = rows
        if send:
            columns = slice(self.sent, stop)
            copy = pltpu.make_async_copy(
                self.source.at[:, columns], self.target.at[:, columns], self.sems.at[len(self.copies)]
            )
            copy.start()
            self.copies.append(copy)
            self.sent = stop

    def finish(self):
        for copy in self.copies:
            copy.wait()


def last_of(i, count, pieces):
    return (i + 1) * pieces // count > i * pieces // count


def write_messages(rank, state, total, sorted_ref, out_refs):
    high, low = split(total)
    for part in range(PARTS):
        rows = state[part * ROWS : (part + 1) * ROWS, :]
        sorted_ref[part] = jnp.concatenate([rows, high.astype(F32), low.astype(F32)], 0)
    for k, out in enumerate(out_refs):
        for i in range(PARTS // 2):
            out[i] = sorted_ref[rank ^ (2 * i + k)].astype(BF16)


def load_state(messages, state):
    for part in range(PARTS):
        state[part * ROWS : (part + 1) * ROWS, :] = messages[part].astype(F32)[:ROWS]


def read_totals(message):
    rows = message[...].astype(F32)
    return rows[ROWS : ROWS + 1], rows[ROWS + 1 : ROWS + 2]


def columns_of(state, block):
    start, stop, low, high, heads = block
    owner = head_of_lane(E, start, stop)
    rows = [jnp.where(owner == h, state[:, start:stop], 0.0) for h in heads]
    before, after = heads[0] * E - low, high - (heads[-1] + 1) * E
    if before > 0:
        rows = [jnp.zeros((before, stop - start), F32)] + rows
    if after > 0:
        rows = rows + [jnp.zeros((after, stop - start), F32)]
    return jnp.concatenate(rows, 0).astype(BF16)


def rows_of(state, block):
    start, stop, low, high, heads = block
    owner = head_of_lane(E, low, high)
    rows = []
    for h in heads:
        first, last = max(start - h * E, 0), min(stop - h * E, E)
        rows.append(jnp.where(owner[first:last] == h, state[first:last, low:high], 0.0))
    return jnp.concatenate(rows, 0).astype(BF16)


def key_kernel(rank_ref, keys_ref, values_ref, *refs):
    out_refs, (state, total, sorted_ref, key_rows, value_rows, sems) = refs[:2], refs[2:]
    tokens, frames, _ = keys_ref.shape
    cuts = [0, tokens // 16 * 8, tokens]
    arrivals = []
    for first, last in zip(cuts, cuts[1:]):
        rows = slice(first * frames, last * frames)
        for source, target in ((keys_ref, key_rows), (values_ref, value_rows)):
            arrivals.append(pltpu.make_async_copy(flat(source).at[rows], target.at[rows], sems.at[len(arrivals)]))
            arrivals[-1].start()
    state[...] = jnp.zeros_like(state)
    total[...] = jnp.zeros_like(total)
    for i, (first, last) in enumerate(zip(cuts, cuts[1:])):
        rows = slice(first * frames, last * frames)
        for copy in arrivals[2 * i : 2 * i + 2]:
            copy.wait()
        feat = jnp.maximum(key_rows[rows], 0)
        add_outer(state, feat, value_rows.at[rows])
        total[...] += dot(jnp.ones((8, feat.shape[0]), BF16), feat, (1, 0))
    write_messages(rank_ref[0], state[...], total[:1], sorted_ref, out_refs)


def renewed(added, total):
    high, low = split(total)
    row = lax.broadcasted_iota(jnp.int32, added.shape, 0)
    added = jnp.where(row == ROWS, high.astype(F32), added)
    return jnp.where(row == ROWS + 1, low.astype(F32), added).astype(BF16)


def total_in(added):
    return added[ROWS : ROWS + 1] + added[ROWS + 1 : ROWS + 2]


def pair_kernel(own_ref, got_ref, *out_refs):
    for i, out in enumerate(out_refs):
        added = own_ref[i].astype(F32) + got_ref[i].astype(F32)
        out[...] = renewed(added, total_in(added))


def sum_kernel(n_total, *refs):
    in_refs, out_ref = refs[:-1], refs[-1]
    in_refs, total_refs = in_refs[: len(in_refs) - n_total], in_refs[len(in_refs) - n_total :]
    added = in_refs[0][...].astype(F32)
    for ref in in_refs[1:]:
        added = added + ref[...].astype(F32)
    out_ref[...] = renewed(added, total_refs[0][:1] if total_refs else total_in(added))


def stack_kernel(*refs):
    for i, ref in enumerate(refs[:-1]):
        refs[-1][i] = ref[...]


def denominator_kernel(queries_ref, message_ref, inverse_ref, spread_ref):
    rows, width = queries_ref.shape
    tot_high, tot_low = read_totals(message_ref)
    denominator = jnp.zeros((rows, 2 * LANES), F32)
    for start, stop, *_ in spans(width):
        row = lax.broadcasted_iota(jnp.int32, (2 * LANES, stop - start), 0)
        tot = jnp.where(row < LANES, tot_high[:, start:stop], tot_low[:, start:stop])
        weights = jnp.where(picks(start, stop, 2 * LANES), tot, 0.0).astype(BF16)
        denominator += dot(jnp.maximum(queries_ref[:, start:stop], 0), weights, (1, 1))
    denominator = denominator[:, :LANES] + denominator[:, LANES:] + EPSILON
    lane = lax.broadcasted_iota(jnp.int32, (rows, LANES), 1)
    inverse = jnp.where(((lane & (COPY - 1)) < H) & (lane < 3 * COPY), 1.0 / denominator, 0.0)
    inverse_ref[...] = inverse
    high = inverse.astype(BF16).astype(F32)
    middle = (inverse - high).astype(BF16).astype(F32)
    low = inverse - high - middle
    spread_ref[...] = jnp.where(lane < COPY, high, jnp.where(lane < 2 * COPY, middle, low)).astype(BF16)


def query_kernel(frames, rank_ref, queries_ref, grad_ref, taps_ref, spread_ref, *refs):
    source_refs, (numer_ref, *refs) = refs[:2], refs[2:]
    out_refs, (state, sorted_ref, next_ref, sems) = refs[:2], refs[2:]
    rows, width = queries_ref.shape
    blocks = spans(width)
    taps = taps_ref[...]
    taps = [taps[0:1] + 1.0, taps[1:2], taps[2:3]]
    state[...] = jnp.zeros_like(state)
    group = 8 if 8 % frames == 0 and rows % 8 == 0 else rows
    cuts, arrivals = sorted({0, 1, min(4, len(blocks)), len(blocks)}), {}
    for k, (begin, end) in enumerate(zip(cuts, cuts[1:])):
        columns, first = slice(blocks[begin][0], blocks[end - 1][1]), 0
        arrivals[begin] = []
        for j, source in enumerate(source_refs):
            last = first + source.shape[0] * frames
            target = next_ref.at[first:last, columns]
            copy = pltpu.make_async_copy(flat(source).at[:, columns], target, sems.at[j, k])
            copy.start()
            arrivals[begin].append(copy)
            first = last
    for i, (start, stop, *_) in enumerate(blocks):
        for copy in arrivals.get(i, ()):
            copy.wait()
        shape = (rows // group, group, stop - start)
        frame = lax.broadcasted_iota(jnp.int32, shape, 1) % frames
        now = grad_ref[:, start:stop].astype(F32).reshape(shape)
        later = next_ref[:, start:stop].astype(F32).reshape(shape)
        upstream = now * taps[0][:, start:stop]
        for lag in (1, 2):
            shifted = later
            if lag < frames:
                mixed = jnp.where(frame >= lag, now, later)
                ahead, behind = pltpu.roll(mixed, group - lag, 1), pltpu.roll(mixed, frames - lag, 1)
                shifted = jnp.where(frame + lag < frames, ahead, behind)
            upstream += shifted * taps[lag][:, start:stop]
        upstream = upstream.reshape(rows, stop - start)
        pick = jnp.where(picks(start, stop), 1.0, 0.0).astype(BF16)
        numer_ref[:, start:stop] = (upstream * dot(spread_ref[...], pick, (1, 0))).astype(BF16)
    add_outer(state, jnp.maximum(queries_ref[...], 0), numer_ref)
    write_messages(rank_ref[0], state[...], jnp.zeros((1, width), F32), sorted_ref, out_refs)


def sort_messages(rank, message_refs, sorted_ref, state):
    for k, stack in enumerate(message_refs):
        for i in range(PARTS // 2):
            sorted_ref[rank ^ (2 * i + k)] = stack[i].astype(F32)
    load_state(sorted_ref, state)


def side_kernel(rank_ref, queries_ref, numer_ref, inverse_ref, *refs):
    message_refs, (sides_ref, total_ref, state, sorted_ref, wide) = refs[:2], refs[2:]
    rows, width = queries_ref.shape
    blocks = spans(width)
    sort_messages(rank_ref[0], message_refs, sorted_ref, state)
    for i, block in enumerate(blocks):
        wide[i, : block[3] - block[2], : block[1] - block[0]] = columns_of(state, block)
    summed = jnp.zeros((rows, LANES), F32)
    for i, (start, stop, low, high, _) in enumerate(blocks):
        pick = jnp.where(picks(start, stop), 1.0, 0.0).astype(BF16)
        feat = jnp.maximum(queries_ref[:, low:high], 0)
        attended = dot(feat, wide[i, : high - low, : stop - start], (1, 0))
        summed += dot((numer_ref[:, start:stop].astype(F32) * attended).astype(BF16), pick, (1, 1))
    high, low = split(-summed * inverse_ref[...])
    high, low = high.astype(F32), low.astype(F32)
    lane = lax.broadcasted_iota(jnp.int32, (rows, LANES), 1)
    sides = jnp.where((lane >= COPY) & (lane < 2 * COPY), low, high)
    pairs = jnp.where(lane < 2 * COPY, sides, 0.0).astype(BF16)
    sides_ref[...] = sides.astype(BF16)
    for start, stop, *_ in blocks:
        terms = dot(pairs, jnp.maximum(queries_ref[:, start:stop], 0), (0, 0))
        terms = jnp.sum(jnp.where(picks(start, stop), terms, 0.0), 0, keepdims=True)
        total_ref[:, start:stop] = jnp.broadcast_to(terms, (8, stop - start))


def query_grad_kernel(scale, rank_ref, queries_ref, numer_ref, sides_ref, *refs):
    message_refs, (out_ref, state, sorted_ref, across, held, sems) = refs[:2], refs[2:]
    blocks = spans(queries_ref.shape[1])
    tot_high, tot_low = read_totals(message_refs[0].at[0])
    sort_messages(rank_ref[0], message_refs, sorted_ref, state)
    for i, block in enumerate(blocks):
        across[i, : block[1] - block[0], : block[3] - block[2]] = rows_of(state, block)
    leaving = Leaving(held, out_ref, sems)
    for i, (start, stop, low, high, _) in enumerate(blocks):
        row = lax.broadcasted_iota(jnp.int32, (LANES, stop - start), 0)
        tot = jnp.where(row < 2 * COPY, tot_high[:, start:stop], tot_low[:, start:stop])
        tot = jnp.where(picks(start, stop), tot, 0.0).astype(BF16)
        grad = dot(numer_ref[:, low:high], across[i, : stop - start, : high - low], (1, 1))
        grad += dot(sides_ref[...], tot, (1, 0))
        grad = jnp.where(queries_ref[:, start:stop].astype(F32) > 0, grad * scale, 0.0).astype(BF16)
        leaving.put(start, stop, grad, last_of(i, len(blocks), 3))
    leaving.finish()


def key_grad_kernel(scale, rank_ref, keys_ref, values_ref, own_ref, got_ref, key_out, value_out, *refs):
    state, sorted_ref, wide, across, key_held, value_held, key_sems, value_sems = refs
    blocks = spans(keys_ref.shape[1])
    sort_messages(rank_ref[0], (own_ref, got_ref), sorted_ref, state)
    rows = sorted_ref[0]
    for part in range(1, PARTS):
        rows = rows + sorted_ref[part]
    row = lax.broadcasted_iota(jnp.int32, rows.shape, 0)
    total = jnp.sum(jnp.where(row >= ROWS, rows, 0.0), 0, keepdims=True)
    key_leaving = Leaving(key_held, key_out, key_sems)
    value_leaving = Leaving(value_held, value_out, value_sems)
    for i, block in enumerate(blocks):
        start, stop, low, high, _ = block
        across[i, : stop - start, : high - low] = rows_of(state, block)
        wide[i, : high - low, : stop - start] = columns_of(state, block)
    for i, (start, stop, low, high, _) in enumerate(blocks):
        grad = dot(values_ref[:, low:high], across[i, : stop - start, : high - low], (1, 1)) + total[:, start:stop]
        alive = keys_ref[:, start:stop].astype(F32) > 0
        grad = jnp.where(alive, grad * scale, 0.0).astype(BF16)
        key_leaving.put(start, stop, grad, last_of(i, len(blocks), 1))
    for i, (start, stop, low, high, _) in enumerate(blocks):
        feat = jnp.maximum(keys_ref[:, low:high], 0)
        grad = dot(feat, wide[i, : high - low, : stop - start], (1, 0))
        value_leaving.put(start, stop, (grad * scale).astype(BF16), last_of(i, len(blocks), 2))
    key_leaving.finish()
    value_leaving.finish()


def cost(flops, size):
    return pl.CostEstimate(flops=flops, bytes_accessed=size, transcendentals=0)


def exchange(block, axis, distance):
    devices = range(lax.axis_size(axis))
    return lax.ppermute(block, axis, [(i, i ^ distance) for i in devices])


def added(parts, total=None):
    totals = [] if total is None else [total]
    return pl.pallas_call(
        functools.partial(sum_kernel, len(totals)),
        out_shape=jax.ShapeDtypeStruct(parts[0].shape, BF16),
        compiler_params=pltpu.CompilerParams(vmem_limit_bytes=8 << 20),
        cost_estimate=cost(0, 9 * 32 * parts[0].shape[1]),
    )(*parts, *totals)


def small(kernel, out_shape, *arrays):
    return pl.pallas_call(
        kernel,
        out_shape=out_shape,
        compiler_params=pltpu.CompilerParams(vmem_limit_bytes=8 << 20),
        cost_estimate=cost(0, 4 * sum(x.size for x in arrays)),
    )(*arrays)


def fan(messages):
    got = [messages[0]]
    for i in range(1, PARTS // 2):
        got.append(exchange(messages[i], "frame", 2 * i))
    return got


def scattered(stacks):
    own, other = stacks
    got = exchange(other, "frame", 1)
    message = jax.ShapeDtypeStruct(own.shape[1:], BF16)
    return fan(small(pair_kernel, [message] * (PARTS // 2), own, got))


def gathered(part):
    parts = fan([part] * (PARTS // 2))
    own = small(stack_kernel, jax.ShapeDtypeStruct((len(parts), *part.shape), BF16), *parts)
    return own, exchange(own, "frame", 1)


def over_groups(part):
    frames = lax.axis_size("frame")
    for axis, steps in (("frame", range(PARTS, frames, PARTS)), ("space", range(1, lax.axis_size("space")))):
        got = []
        for d in steps:
            got.append(exchange(part, axis, d))
        if got:
            part = added([part, *got])
    return part


def shards(grad_out, conv_taps, saved_queries, saved_keys, saved_values):
    frames, tokens, width = grad_out.shape
    devices = lax.axis_size("frame")
    rank = (lax.axis_index("frame") % PARTS).astype(jnp.int32).reshape(1)
    scale = 2.0 * math.sqrt(frames * devices * tokens * lax.axis_size("space"))
    grad_out, saved_queries, saved_keys, saved_values = (
        x.transpose(1, 0, 2) for x in (grad_out, saved_queries, saved_keys, saved_values)
    )
    array = jax.ShapeDtypeStruct(grad_out.shape, BF16)
    stack = jax.ShapeDtypeStruct((PARTS // 2, ROWS + 2, width), BF16)
    smem = pl.BlockSpec(memory_space=pltpu.SMEM)
    vmem = pl.BlockSpec(memory_space=pltpu.VMEM)
    window = max(block[3] - block[2] for block in spans(width))
    state = pltpu.VMEM((E, width), F32)
    ordered = pltpu.VMEM((PARTS, ROWS + 2, width), F32)
    across = pltpu.VMEM((len(spans(width)), SPAN, window), BF16)
    wide = pltpu.VMEM((len(spans(width)), window, SPAN), BF16)
    size = 2 * frames * tokens * width

    anywhere = pl.BlockSpec(memory_space=pl.ANY)
    merged = jax.ShapeDtypeStruct((frames * tokens, width), BF16)
    held = pltpu.VMEM(merged.shape, BF16)
    sems = pltpu.SemaphoreType.DMA((len(spans(width)),))

    def relay(*sources):
        return pl.pallas_call(
            relay_kernel,
            in_specs=[anywhere] * len(sources),
            out_specs=[vmem] * len(sources),
            out_shape=[merged] * len(sources),
            scratch_shapes=[pltpu.SemaphoreType.DMA((len(sources),))],
            compiler_params=PARAMS,
            cost_estimate=cost(0, 2 * size * len(sources)),
        )(*sources)

    def halo(source):
        return lax.ppermute(source, "frame", [(i + 1, i) for i in range(devices - 1)])

    early = tokens * 40 // 100 // 8 * 8
    following = [halo(grad_out[:early])]
    key = pl.pallas_call(
        key_kernel,
        in_specs=[smem, anywhere, anywhere],
        out_specs=[vmem] * 2,
        out_shape=[stack] * 2,
        scratch_shapes=[state, pltpu.VMEM((8, width), F32), ordered, held, held, pltpu.SemaphoreType.DMA((4,))],
        compiler_params=LARGE,
        cost_estimate=cost(size * 512, 2 * size),
    )
    state_messages = key(rank, saved_keys, saved_values)
    following.append(halo(grad_out[early:]))
    query_rows, grad_rows = relay(saved_queries, grad_out)
    part = over_groups(added(scattered(state_messages)))
    per_head = (frames * tokens, LANES)
    denominators = pl.pallas_call(
        denominator_kernel,
        out_shape=[jax.ShapeDtypeStruct(per_head, F32), jax.ShapeDtypeStruct(per_head, BF16)],
        compiler_params=PARAMS,
        cost_estimate=cost(size * 128, size),
    )
    inverse, spread = denominators(query_rows, part)
    query = pl.pallas_call(
        functools.partial(query_kernel, frames),
        in_specs=[smem] + [vmem] * 4 + [anywhere] * 2,
        out_shape=[merged] + [stack] * 2,
        scratch_shapes=[state, ordered, held, pltpu.SemaphoreType.DMA((2, len(spans(width))))],
        compiler_params=PARAMS,
        cost_estimate=cost(size * 1024, 4 * size),
    )
    numer, *grad_messages = query(rank, query_rows, grad_rows, conv_taps, spread, *following)
    states = gathered(part)
    grad_parts = scattered(grad_messages)
    side = pl.pallas_call(
        side_kernel,
        in_specs=[smem] + [vmem] * 5,
        out_shape=[jax.ShapeDtypeStruct(per_head, BF16), jax.ShapeDtypeStruct((8, width), F32)],
        scratch_shapes=[state, ordered, wide],
        compiler_params=PARAMS,
        cost_estimate=cost(size * 512, 2 * size),
    )
    sides, total = side(rank, query_rows, numer, inverse, *states)
    query_grad = pl.pallas_call(
        functools.partial(query_grad_kernel, scale),
        in_specs=[smem] + [vmem] * 5,
        out_specs=anywhere,
        out_shape=array,
        scratch_shapes=[state, ordered, across, held, sems],
        compiler_params=PARAMS,
        cost_estimate=cost(size * 512, 3 * size),
    )
    grad_queries = query_grad(rank, query_rows, numer, sides, *states)
    key_rows, value_rows = relay(saved_keys, saved_values)
    part = over_groups(added(grad_parts, total))
    grads = gathered(part)
    grad_keys, grad_values = pl.pallas_call(
        functools.partial(key_grad_kernel, scale),
        in_specs=[smem] + [vmem] * 4,
        out_specs=[anywhere] * 2,
        out_shape=[array, array],
        scratch_shapes=[state, ordered, wide, across, held, held, sems, sems],
        compiler_params=PARAMS,
        cost_estimate=cost(size * 1024, 4 * size),
    )(rank, key_rows, value_rows, *grads)
    return tuple(x.transpose(1, 0, 2) for x in (grad_queries, grad_keys, grad_values))


def solution(mesh):
    block = P("frame", "space", None)
    return jax.shard_map(
        shards,
        mesh=mesh,
        in_specs=(block, P(), block, block, block),
        out_specs=(block, block, block),
        check_vma=False,
    )
```

```python
import functools
import math

import jax
import jax.numpy as jnp
from jax import lax
from jax.experimental import pallas as pl
from jax.experimental.pallas import tpu as pltpu
from jax.sharding import PartitionSpec as P


H = 20
E = 112
EPSILON = 1e-06
LANES = 128
SPAN = 256
ROWS = 14
PARTS = E // ROWS
COPY = 32
F32, BF16 = jnp.float32, jnp.bfloat16
LARGE = pltpu.CompilerParams(vmem_limit_bytes=57 << 20)
PARAMS = pltpu.CompilerParams(vmem_limit_bytes=24 << 20)


def spans(width):
    blocks = []
    for start in range(0, width, SPAN):
        stop = min(start + SPAN, width)
        first, last = start // E, (stop - 1) // E
        low = first * E // LANES * LANES
        high = min(-(-(last + 1) * E // LANES) * LANES, width)
        blocks.append((start, stop, low, high, range(first, last + 1)))
    return blocks


def dot(a, b, contract):
    return lax.dot_general(a, b, ((contract[:1], contract[1:]), ((), ())), preferred_element_type=F32)


def head_of_lane(rows, start, stop):
    lane = lax.broadcasted_iota(jnp.int32, (1, stop - start), 1) + start
    head = jnp.full((1, stop - start), start // E, jnp.int32)
    for h in range(start // E + 1, (stop - 1) // E + 1):
        head += (lane >= h * E).astype(jnp.int32)
    return jnp.broadcast_to(head, (rows, stop - start))


def picks(start, stop, rows=LANES):
    row = lax.broadcasted_iota(jnp.int32, (rows, 1), 0) & (LANES - 1)
    slot = jnp.where(row < 3 * COPY, row & (COPY - 1), -1)
    return jnp.broadcast_to(slot, (rows, stop - start)) == head_of_lane(rows, start, stop)


def split(x):
    high = x.astype(BF16)
    return high, (x - high.astype(F32)).astype(BF16)


def add_outer(state, left, right):
    for start, stop, low, high, heads in spans(left.shape[1]):
        product = dot(left[:, low:high], right[:, start:stop], (0, 0))
        owner = head_of_lane(E, start, stop)
        part = jnp.zeros((E, stop - start), F32)
        for h in heads:
            part = jnp.where(owner == h, product[h * E - low : (h + 1) * E - low], part)
        state[:, start:stop] += part


def flat(ref):
    tokens, frames, width = ref.shape
    return ref.reshape(tokens * frames, width)


def relay_kernel(*refs):
    count = len(refs) // 2
    in_refs, out_refs, sems = refs[:count], refs[count : 2 * count], refs[2 * count]
    copies = [
        pltpu.make_async_copy(flat(source), target, sems.at[i])
        for i, (source, target) in enumerate(zip(in_refs, out_refs))
    ]
    for copy in copies:
        copy.start()
    for copy in copies:
        copy.wait()


class Leaving:
    def __init__(self, source, target, sems):
        self.source, self.target, self.sems, self.copies, self.sent = source, flat(target), sems, [], 0

    def put(self, start, stop, rows, send):
        self.source[:, start:stop] = rows
        if send:
            columns = slice(self.sent, stop)
            copy = pltpu.make_async_copy(
                self.source.at[:, columns], self.target.at[:, columns], self.sems.at[len(self.copies)]
            )
            copy.start()
            self.copies.append(copy)
            self.sent = stop

    def finish(self):
        for copy in self.copies:
            copy.wait()


def last_of(i, count, pieces):
    return (i + 1) * pieces // count > i * pieces // count


def write_messages(rank, state, total, sorted_ref, out_refs):
    high, low = split(total)
    for part in range(PARTS):
        rows = state[part * ROWS : (part + 1) * ROWS, :]
        sorted_ref[part] = jnp.concatenate([rows, high.astype(F32), low.astype(F32)], 0)
    for k, out in enumerate(out_refs):
        for i in range(PARTS // 2):
            out[i] = sorted_ref[rank ^ (2 * i + k)].astype(BF16)


def load_state(messages, state):
    for part in range(PARTS):
        state[part * ROWS : (part + 1) * ROWS, :] = messages[part].astype(F32)[:ROWS]


def read_totals(message):
    rows = message[...].astype(F32)
    return rows[ROWS : ROWS + 1], rows[ROWS + 1 : ROWS + 2]


def columns_of(state, block):
    start, stop, low, high, heads = block
    owner = head_of_lane(E, start, stop)
    rows = [jnp.where(owner == h, state[:, start:stop], 0.0) for h in heads]
    before, after = heads[0] * E - low, high - (heads[-1] + 1) * E
    if before > 0:
        rows = [jnp.zeros((before, stop - start), F32)] + rows
    if after > 0:
        rows = rows + [jnp.zeros((after, stop - start), F32)]
    return jnp.concatenate(rows, 0).astype(BF16)


def rows_of(state, block):
    start, stop, low, high, heads = block
    owner = head_of_lane(E, low, high)
    rows = []
    for h in heads:
        first, last = max(start - h * E, 0), min(stop - h * E, E)
        rows.append(jnp.where(owner[first:last] == h, state[first:last, low:high], 0.0))
    return jnp.concatenate(rows, 0).astype(BF16)


def key_kernel(rank_ref, keys_ref, values_ref, *refs):
    out_refs, (state, total, sorted_ref, key_rows, value_rows, sems) = refs[:2], refs[2:]
    tokens, frames, _ = keys_ref.shape
    cuts = [0, tokens // 16 * 8, tokens]
    arrivals = []
    for first, last in zip(cuts, cuts[1:]):
        rows = slice(first * frames, last * frames)
        for source, target in ((keys_ref, key_rows), (values_ref, value_rows)):
            arrivals.append(pltpu.make_async_copy(flat(source).at[rows], target.at[rows], sems.at[len(arrivals)]))
            arrivals[-1].start()
    state[...] = jnp.zeros_like(state)
    total[...] = jnp.zeros_like(total)
    for i, (first, last) in enumerate(zip(cuts, cuts[1:])):
        rows = slice(first * frames, last * frames)
        for copy in arrivals[2 * i : 2 * i + 2]:
            copy.wait()
        feat = jnp.maximum(key_rows[rows], 0)
        add_outer(state, feat, value_rows.at[rows])
        total[...] += dot(jnp.ones((8, feat.shape[0]), BF16), feat, (1, 0))
    write_messages(rank_ref[0], state[...], total[:1], sorted_ref, out_refs)


def renewed(added, total):
    high, low = split(total)
    row = lax.broadcasted_iota(jnp.int32, added.shape, 0)
    added = jnp.where(row == ROWS, high.astype(F32), added)
    return jnp.where(row == ROWS + 1, low.astype(F32), added).astype(BF16)


def total_in(added):
    return added[ROWS : ROWS + 1] + added[ROWS + 1 : ROWS + 2]


def pair_kernel(own_ref, got_ref, *out_refs):
    for i, out in enumerate(out_refs):
        added = own_ref[i].astype(F32) + got_ref[i].astype(F32)
        out[...] = renewed(added, total_in(added))


def sum_kernel(n_total, *refs):
    in_refs, out_ref = refs[:-1], refs[-1]
    in_refs, total_refs = in_refs[: len(in_refs) - n_total], in_refs[len(in_refs) - n_total :]
    added = in_refs[0][...].astype(F32)
    for ref in in_refs[1:]:
        added = added + ref[...].astype(F32)
    out_ref[...] = renewed(added, total_refs[0][:1] if total_refs else total_in(added))


def stack_kernel(*refs):
    for i, ref in enumerate(refs[:-1]):
        refs[-1][i] = ref[...]


def denominator_kernel(queries_ref, message_ref, inverse_ref, spread_ref):
    rows, width = queries_ref.shape
    tot_high, tot_low = read_totals(message_ref)
    denominator = jnp.zeros((rows, 2 * LANES), F32)
    for start, stop, *_ in spans(width):
        row = lax.broadcasted_iota(jnp.int32, (2 * LANES, stop - start), 0)
        tot = jnp.where(row < LANES, tot_high[:, start:stop], tot_low[:, start:stop])
        weights = jnp.where(picks(start, stop, 2 * LANES), tot, 0.0).astype(BF16)
        denominator += dot(jnp.maximum(queries_ref[:, start:stop], 0), weights, (1, 1))
    denominator = denominator[:, :LANES] + denominator[:, LANES:] + EPSILON
    lane = lax.broadcasted_iota(jnp.int32, (rows, LANES), 1)
    inverse = jnp.where(((lane & (COPY - 1)) < H) & (lane < 3 * COPY), 1.0 / denominator, 0.0)
    inverse_ref[...] = inverse
    high = inverse.astype(BF16).astype(F32)
    middle = (inverse - high).astype(BF16).astype(F32)
    low = inverse - high - middle
    spread_ref[...] = jnp.where(lane < COPY, high, jnp.where(lane < 2 * COPY, middle, low)).astype(BF16)


def query_kernel(frames, rank_ref, queries_ref, grad_ref, taps_ref, spread_ref, *refs):
    source_refs, (numer_ref, *refs) = refs[:2], refs[2:]
    out_refs, (state, sorted_ref, next_ref, sems) = refs[:2], refs[2:]
    rows, width = queries_ref.shape
    blocks = spans(width)
    taps = taps_ref[...]
    taps = [taps[0:1] + 1.0, taps[1:2], taps[2:3]]
    state[...] = jnp.zeros_like(state)
    group = 8 if 8 % frames == 0 and rows % 8 == 0 else rows
    cuts, arrivals = sorted({0, min(2, len(blocks)), len(blocks)}), {}
    for k, (begin, end) in enumerate(zip(cuts, cuts[1:])):
        columns, first = slice(blocks[begin][0], blocks[end - 1][1]), 0
        arrivals[begin] = []
        for j, source in enumerate(source_refs):
            last = first + source.shape[0] * frames
            target = next_ref.at[first:last, columns]
            copy = pltpu.make_async_copy(flat(source).at[:, columns], target, sems.at[j, k])
            copy.start()
            arrivals[begin].append(copy)
            first = last
    for i, (start, stop, *_) in enumerate(blocks):
        for copy in arrivals.get(i, ()):
            copy.wait()
        shape = (rows // group, group, stop - start)
        frame = lax.broadcasted_iota(jnp.int32, shape, 1) % frames
        now = grad_ref[:, start:stop].astype(F32).reshape(shape)
        later = next_ref[:, start:stop].astype(F32).reshape(shape)
        upstream = now * taps[0][:, start:stop]
        for lag in (1, 2):
            shifted = later
            if lag < frames:
                mixed = jnp.where(frame >= lag, now, later)
                ahead, behind = pltpu.roll(mixed, group - lag, 1), pltpu.roll(mixed, frames - lag, 1)
                shifted = jnp.where(frame + lag < frames, ahead, behind)
            upstream += shifted * taps[lag][:, start:stop]
        upstream = upstream.reshape(rows, stop - start)
        pick = jnp.where(picks(start, stop), 1.0, 0.0).astype(BF16)
        numer_ref[:, start:stop] = (upstream * dot(spread_ref[...], pick, (1, 0))).astype(BF16)
    add_outer(state, jnp.maximum(queries_ref[...], 0), numer_ref)
    write_messages(rank_ref[0], state[...], jnp.zeros((1, width), F32), sorted_ref, out_refs)


def sort_messages(rank, message_refs, sorted_ref, state):
    for k, stack in enumerate(message_refs):
        for i in range(PARTS // 2):
            sorted_ref[rank ^ (2 * i + k)] = stack[i].astype(F32)
    load_state(sorted_ref, state)


def side_kernel(rank_ref, queries_ref, numer_ref, inverse_ref, *refs):
    message_refs, (sides_ref, total_ref, state, sorted_ref, wide) = refs[:2], refs[2:]
    rows, width = queries_ref.shape
    blocks = spans(width)
    sort_messages(rank_ref[0], message_refs, sorted_ref, state)
    for i, block in enumerate(blocks):
        wide[i, : block[3] - block[2], : block[1] - block[0]] = columns_of(state, block)
    summed = jnp.zeros((rows, LANES), F32)
    for i, (start, stop, low, high, _) in enumerate(blocks):
        pick = jnp.where(picks(start, stop), 1.0, 0.0).astype(BF16)
        feat = jnp.maximum(queries_ref[:, low:high], 0)
        attended = dot(feat, wide[i, : high - low, : stop - start], (1, 0))
        summed += dot((numer_ref[:, start:stop].astype(F32) * attended).astype(BF16), pick, (1, 1))
    high, low = split(-summed * inverse_ref[...])
    high, low = high.astype(F32), low.astype(F32)
    lane = lax.broadcasted_iota(jnp.int32, (rows, LANES), 1)
    sides = jnp.where((lane >= COPY) & (lane < 2 * COPY), low, high)
    pairs = jnp.where(lane < 2 * COPY, sides, 0.0).astype(BF16)
    sides_ref[...] = sides.astype(BF16)
    for start, stop, *_ in blocks:
        terms = dot(pairs, jnp.maximum(queries_ref[:, start:stop], 0), (0, 0))
        terms = jnp.sum(jnp.where(picks(start, stop), terms, 0.0), 0, keepdims=True)
        total_ref[:, start:stop] = jnp.broadcast_to(terms, (8, stop - start))


def query_grad_kernel(scale, rank_ref, queries_ref, numer_ref, sides_ref, *refs):
    message_refs, (out_ref, state, sorted_ref, across, held, sems) = refs[:2], refs[2:]
    blocks = spans(queries_ref.shape[1])
    tot_high, tot_low = read_totals(message_refs[0].at[0])
    sort_messages(rank_ref[0], message_refs, sorted_ref, state)
    for i, block in enumerate(blocks):
        across[i, : block[1] - block[0], : block[3] - block[2]] = rows_of(state, block)
    leaving = Leaving(held, out_ref, sems)
    for i, (start, stop, low, high, _) in enumerate(blocks):
        row = lax.broadcasted_iota(jnp.int32, (LANES, stop - start), 0)
        tot = jnp.where(row < 2 * COPY, tot_high[:, start:stop], tot_low[:, start:stop])
        tot = jnp.where(picks(start, stop), tot, 0.0).astype(BF16)
        grad = dot(numer_ref[:, low:high], across[i, : stop - start, : high - low], (1, 1))
        grad += dot(sides_ref[...], tot, (1, 0))
        grad = jnp.where(queries_ref[:, start:stop].astype(F32) > 0, grad * scale, 0.0).astype(BF16)
        leaving.put(start, stop, grad, last_of(i, len(blocks), 2))
    leaving.finish()


def key_grad_kernel(scale, rank_ref, keys_ref, values_ref, own_ref, got_ref, key_out, value_out, *refs):
    state, sorted_ref, wide, across, key_held, value_held, key_sems, value_sems = refs
    blocks = spans(keys_ref.shape[1])
    sort_messages(rank_ref[0], (own_ref, got_ref), sorted_ref, state)
    rows = sorted_ref[0]
    for part in range(1, PARTS):
        rows = rows + sorted_ref[part]
    row = lax.broadcasted_iota(jnp.int32, rows.shape, 0)
    total = jnp.sum(jnp.where(row >= ROWS, rows, 0.0), 0, keepdims=True)
    key_leaving = Leaving(key_held, key_out, key_sems)
    value_leaving = Leaving(value_held, value_out, value_sems)
    for i, block in enumerate(blocks):
        start, stop, low, high, _ = block
        across[i, : stop - start, : high - low] = rows_of(state, block)
        wide[i, : high - low, : stop - start] = columns_of(state, block)
    for i, (start, stop, low, high, _) in enumerate(blocks):
        grad = dot(values_ref[:, low:high], across[i, : stop - start, : high - low], (1, 1)) + total[:, start:stop]
        alive = keys_ref[:, start:stop].astype(F32) > 0
        grad = jnp.where(alive, grad * scale, 0.0).astype(BF16)
        key_leaving.put(start, stop, grad, last_of(i, len(blocks), 1))
    for i, (start, stop, low, high, _) in enumerate(blocks):
        feat = jnp.maximum(keys_ref[:, low:high], 0)
        grad = dot(feat, wide[i, : high - low, : stop - start], (1, 0))
        value_leaving.put(start, stop, (grad * scale).astype(BF16), i in (len(blocks) * 2 // 3, len(blocks) - 1))
    key_leaving.finish()
    value_leaving.finish()


def cost(flops, size):
    return pl.CostEstimate(flops=flops, bytes_accessed=size, transcendentals=0)


def exchange(block, axis, distance):
    devices = range(lax.axis_size(axis))
    return lax.ppermute(block, axis, [(i, i ^ distance) for i in devices])


def added(parts, total=None):
    totals = [] if total is None else [total]
    return pl.pallas_call(
        functools.partial(sum_kernel, len(totals)),
        out_shape=jax.ShapeDtypeStruct(parts[0].shape, BF16),
        compiler_params=pltpu.CompilerParams(vmem_limit_bytes=8 << 20),
        cost_estimate=cost(0, 9 * 32 * parts[0].shape[1]),
    )(*parts, *totals)


def small(kernel, out_shape, *arrays):
    return pl.pallas_call(
        kernel,
        out_shape=out_shape,
        compiler_params=pltpu.CompilerParams(vmem_limit_bytes=8 << 20),
        cost_estimate=cost(0, 4 * sum(x.size for x in arrays)),
    )(*arrays)


def fan(messages):
    got = [messages[0]]
    for i in range(1, PARTS // 2):
        got.append(exchange(messages[i], "frame", 2 * i))
    return got


def scattered(stacks):
    own, other = stacks
    got = exchange(other, "frame", 1)
    message = jax.ShapeDtypeStruct(own.shape[1:], BF16)
    return fan(small(pair_kernel, [message] * (PARTS // 2), own, got))


def gathered(part):
    parts = fan([part] * (PARTS // 2))
    own = small(stack_kernel, jax.ShapeDtypeStruct((len(parts), *part.shape), BF16), *parts)
    return own, exchange(own, "frame", 1)


def over_groups(part):
    frames = lax.axis_size("frame")
    for axis, steps in (("frame", range(PARTS, frames, PARTS)), ("space", range(1, lax.axis_size("space")))):
        got = []
        for d in steps:
            got.append(exchange(part, axis, d))
        if got:
            part = added([part, *got])
    return part


def shards(grad_out, conv_taps, saved_queries, saved_keys, saved_values):
    frames, tokens, width = grad_out.shape
    devices = lax.axis_size("frame")
    rank = (lax.axis_index("frame") % PARTS).astype(jnp.int32).reshape(1)
    scale = 2.0 * math.sqrt(frames * devices * tokens * lax.axis_size("space"))
    grad_out, saved_queries, saved_keys, saved_values = (
        x.transpose(1, 0, 2) for x in (grad_out, saved_queries, saved_keys, saved_values)
    )
    array = jax.ShapeDtypeStruct(grad_out.shape, BF16)
    stack = jax.ShapeDtypeStruct((PARTS // 2, ROWS + 2, width), BF16)
    smem = pl.BlockSpec(memory_space=pltpu.SMEM)
    vmem = pl.BlockSpec(memory_space=pltpu.VMEM)
    window = max(block[3] - block[2] for block in spans(width))
    state = pltpu.VMEM((E, width), F32)
    ordered = pltpu.VMEM((PARTS, ROWS + 2, width), F32)
    across = pltpu.VMEM((len(spans(width)), SPAN, window), BF16)
    wide = pltpu.VMEM((len(spans(width)), window, SPAN), BF16)
    size = 2 * frames * tokens * width

    anywhere = pl.BlockSpec(memory_space=pl.ANY)
    merged = jax.ShapeDtypeStruct((frames * tokens, width), BF16)
    held = pltpu.VMEM(merged.shape, BF16)
    sems = pltpu.SemaphoreType.DMA((len(spans(width)),))

    def relay(*sources):
        return pl.pallas_call(
            relay_kernel,
            in_specs=[anywhere] * len(sources),
            out_specs=[vmem] * len(sources),
            out_shape=[merged] * len(sources),
            scratch_shapes=[pltpu.SemaphoreType.DMA((len(sources),))],
            compiler_params=PARAMS,
            cost_estimate=cost(0, 2 * size * len(sources)),
        )(*sources)

    def halo(source):
        return lax.ppermute(source, "frame", [(i + 1, i) for i in range(devices - 1)])

    early = tokens * 40 // 100 // 8 * 8
    following = [halo(grad_out[:early])]
    key = pl.pallas_call(
        key_kernel,
        in_specs=[smem, anywhere, anywhere],
        out_specs=[vmem] * 2,
        out_shape=[stack] * 2,
        scratch_shapes=[state, pltpu.VMEM((8, width), F32), ordered, held, held, pltpu.SemaphoreType.DMA((4,))],
        compiler_params=LARGE,
        cost_estimate=cost(size * 512, 2 * size),
    )
    state_messages = key(rank, saved_keys, saved_values)
    following.append(halo(grad_out[early:]))
    query_rows, grad_rows = relay(saved_queries, grad_out)
    part = over_groups(added(scattered(state_messages)))
    per_head = (frames * tokens, LANES)
    denominators = pl.pallas_call(
        denominator_kernel,
        out_shape=[jax.ShapeDtypeStruct(per_head, F32), jax.ShapeDtypeStruct(per_head, BF16)],
        compiler_params=PARAMS,
        cost_estimate=cost(size * 128, size),
    )
    inverse, spread = denominators(query_rows, part)
    query = pl.pallas_call(
        functools.partial(query_kernel, frames),
        in_specs=[smem] + [vmem] * 4 + [anywhere] * 2,
        out_shape=[merged] + [stack] * 2,
        scratch_shapes=[state, ordered, held, pltpu.SemaphoreType.DMA((2, len(spans(width))))],
        compiler_params=PARAMS,
        cost_estimate=cost(size * 1024, 4 * size),
    )
    numer, *grad_messages = query(rank, query_rows, grad_rows, conv_taps, spread, *following)
    states = gathered(part)
    grad_parts = scattered(grad_messages)
    side = pl.pallas_call(
        side_kernel,
        in_specs=[smem] + [vmem] * 5,
        out_shape=[jax.ShapeDtypeStruct(per_head, BF16), jax.ShapeDtypeStruct((8, width), F32)],
        scratch_shapes=[state, ordered, wide],
        compiler_params=PARAMS,
        cost_estimate=cost(size * 512, 2 * size),
    )
    sides, total = side(rank, query_rows, numer, inverse, *states)
    query_grad = pl.pallas_call(
        functools.partial(query_grad_kernel, scale),
        in_specs=[smem] + [vmem] * 5,
        out_specs=anywhere,
        out_shape=array,
        scratch_shapes=[state, ordered, across, held, sems],
        compiler_params=PARAMS,
        cost_estimate=cost(size * 512, 3 * size),
    )
    grad_queries = query_grad(rank, query_rows, numer, sides, *states)
    key_rows, value_rows = relay(saved_keys, saved_values)
    part = over_groups(added(grad_parts, total))
    grads = gathered(part)
    grad_keys, grad_values = pl.pallas_call(
        functools.partial(key_grad_kernel, scale),
        in_specs=[smem] + [vmem] * 4,
        out_specs=[anywhere] * 2,
        out_shape=[array, array],
        scratch_shapes=[state, ordered, wide, across, held, held, sems, sems],
        compiler_params=PARAMS,
        cost_estimate=cost(size * 1024, 4 * size),
    )(rank, key_rows, value_rows, *grads)
    return tuple(x.transpose(1, 0, 2) for x in (grad_queries, grad_keys, grad_values))


def solution(mesh):
    block = P("frame", "space", None)
    return jax.shard_map(
        shards,
        mesh=mesh,
        in_specs=(block, P(), block, block, block),
        out_specs=(block, block, block),
        check_vma=False,
    )
```
